32 devices in a mesh: group: 2 (over x), tile: 16 (over z, y, core).
Axes of the slice: x: 2, y: 2, z: 4, core: 2. Of those that a mesh axis runs over, the one named last changes fastest.
Arguments:
- residual: bfloat16 [4096, 128], P(('group', 'tile')), parts along dimension 0, may hold values from -6 to 6
- chosen: int32 [512], P(('group', 'tile')), parts along dimension 0, may hold values 0 or 1
- footprint_tile: int32 [2048, 4], P('tile'), may hold values from 0 to 15, all different within a row; in each aligned block of 128 rows (0 to 127, 128 to 255, ...) at most 32 rows name the same one
- footprint_block: int32 [2048, 4], P('tile'), may hold values from 0 to 6143
- interp: float32 [128, 128], replicated, may hold values from -0.5 to 0.5
- speed: float32 [64, 384, 512], P('tile'), may hold values from 0.25 to 1
Outputs:
- adjoint_field: float32 [128, 384, 512], P(('group', 'tile')), parts along dimension 0
- partials: float32 [4096, 128], P(('group', 'tile')), parts along dimension 0
The draws below stay inside these ranges and needn't reach their ends.
There are 2 independent parts, one for each index of `group`. The reference program is written for one: setup_inputs(seed, part) draws one part's arguments, and reference() takes and returns one part's arrays. A program takes and returns all parts, laid end to end along the dimension named above; an argument that names none is the same for every part. Nothing has to cross between parts.
Inputs may be any that keep to these rules, and one draw needn't show every extreme that they name: `footprint_tile`: the 4 tiles of a row differ; within the rows of one device no tile is named by more than 32 rows, a bound that some block reaches.
All inputs are finite; a program needn't handle non-finite values. No bound on the sum of `chosen` on one device may be relied on, other than what follows from the above.
Results may differ from the reference program's by a relative error of at most 0.0014.
Values may be sent and summed in bfloat16 or wider, within the bound.
A program may use at most 128 MiB of HBM per device.

```python
import math
import jax
import jax.numpy as jnp
import numpy as np
from jax import lax

SAMP = 128
NBLK = 8
TOP = 4
CAP = 32
STEPS = 4
NY = 384
NZ = 512
SENSORS = 256
ROWS_DEV = 128
ROWS = 2048
NX = 64
CBLK = 6144
N_TILE = 16


def plant(drawn, stream_key, smallest, high):
    dims = drawn.shape
    index_at = [jax.random.randint(jax.random.fold_in(stream_key, axis), (), 0, dims[axis]) for axis in range(len(dims))]
    drawn = drawn.at[tuple(index_at)].set(smallest)
    longest = dims.index(max(dims))
    index_at[longest] = (index_at[longest] + 1) % dims[longest]
    return drawn.at[tuple(index_at)].set(high)


def block_scale(rng, extent, cuts, smallest, top_value):
    factor_of, own = 1.0, jax.random.fold_in(rng, 6)
    for dim, parts in cuts:
        heights = jnp.exp(jax.random.uniform(jax.random.fold_in(own, dim), (parts,), jnp.float32, smallest / len(cuts), top_value / len(cuts)))
        factor_of = factor_of * jnp.repeat(heights, extent[dim] // parts).reshape([-1 if axis == dim else 1 for axis in range(len(extent))])
    return factor_of


def routed_block(rng, own, number, rows, number_of, top, most, skew):
    sequence = jax.random.permutation(rng, number_of)
    heavy_load, common = shares(number_of, rows * top, most, skew, True), shares(number_of, rows * top, most, skew, False)
    places = jnp.arange(number_of)

    def named(lengths, rotation):
        used = int((lengths > 0).sum())
        fixed = max(1, used // 4)
        shifted = fixed + (places - fixed + rotation * (used - fixed)) % max(1, number_of - fixed)
        return jnp.zeros((number_of,), jnp.int32).at[sequence[jnp.where(places < fixed, places, shifted)]].set(jnp.asarray(lengths, jnp.int32))

    lengths = jnp.where(number % 4 == 0, named(heavy_load, number // 4), named(common, number - number // 4 - 1))
    mixed = jax.random.permutation(jax.random.fold_in(own, 3), number_of)
    source_of, sink = mixed[0:number_of // 2 * 2:2], mixed[1:number_of // 2 * 2:2]
    slack = jnp.minimum(lengths[source_of] - 1, most - lengths[sink]) // 2
    slack = jnp.where((source_of == sequence[0]) | (sink == sequence[0]) | (lengths[sink] == 0), 0, jnp.maximum(slack, 0))
    shifted = jax.random.randint(jax.random.fold_in(own, 4), (number_of // 2,), 0, 1 << 20) % (slack + 1)
    lengths = lengths.at[source_of].add(-shifted).at[sink].add(shifted)
    items = jnp.searchsorted(jnp.cumsum(lengths), jnp.arange(rows * top), side="right").astype(jnp.int32)
    listing = items.reshape(top, rows).T
    listing = listing[jax.random.permutation(jax.random.fold_in(own, 1), rows)]
    rotation = jax.random.randint(jax.random.fold_in(own, 2), (rows, 1), 0, top)
    return jnp.take_along_axis(listing, (jnp.arange(top)[None, :] + rotation) % top, axis=1)


def shares(number_of, total, most, lean, full):
    portions = [(1 << 20) // math.isqrt(standing ** lean) + 1 for standing in range(1, number_of + 1)]
    largest = most if full else min(most, max(-(-total // number_of), total * portions[0] // sum(portions)))
    least = 1 if total - largest >= number_of - 1 else 0
    given, surplus = [largest] + [least] * (number_of - 1), total - largest - least * (number_of - 1)
    while surplus > 0:
        movable = [i for i in range(1, number_of) if given[i] < largest] or [i for i in range(1, number_of) if given[i] < most]
        mass, remaining = sum([portions[i] for i in movable]), surplus
        for i in movable:
            addition = min(most - given[i], max(1, remaining * portions[i] // mass), surplus)
            given[i] = given[i] + addition
            surplus = surplus - addition
    return np.array(given)


def scatter_about(rng, dims, scale, bound, pieces=(), dtype=jnp.bfloat16):
    loudness = block_scale(rng, dims, pieces, -0.22, 0.18) if pieces else 1.0
    drawn = jax.random.normal(rng, dims, jnp.float32) * scale * loudness
    return jnp.minimum(jnp.maximum(drawn, -bound), bound).astype(dtype)


def setup_inputs(seed: int = 0, part: int = 0) -> dict:
    streams_of = jax.random.split(jax.random.key(seed), 7)
    own_keys = jax.random.split(jax.random.fold_in(streams_of[6], part), 7)
    residual = scatter_about(own_keys[0], (ROWS, SAMP), 1.0, 6.0, ((0, 16),))
    chosen = plant((jax.random.randint(own_keys[1], (SENSORS,), 0, 2) < 1).astype(jnp.int32), jax.random.fold_in(own_keys[1], 1), 0, 1)
    footprint_tile_keys = jax.random.split(jax.random.fold_in(streams_of[2], 1), ROWS // ROWS_DEV)
    footprint_tile_turns = jax.random.permutation(jax.random.fold_in(streams_of[2], 3), ROWS // ROWS_DEV)
    footprint_tile = jax.vmap(lambda own, number: routed_block(jax.random.fold_in(streams_of[2], 2), own, number, ROWS_DEV, N_TILE, TOP, CAP, 2))(footprint_tile_keys, footprint_tile_turns).reshape((ROWS, TOP))
    footprint_block = plant(jax.random.randint(streams_of[3], (ROWS, TOP), 0, CBLK), jax.random.fold_in(streams_of[3], 1), 0, CBLK - 1).astype(jnp.int32)
    interp = scatter_about(streams_of[4], (SAMP, SAMP), SAMP ** -0.5, 0.5, (), jnp.float32)
    speed = jnp.clip(jnp.exp(math.log(1.0) - 1.3862944 * jax.random.uniform(streams_of[5], (NX, NY, NZ), jnp.float32) ** block_scale(streams_of[5], (NX, NY, NZ), ((0, 16),), -0.2, 0.2)), 0.25, 1.0)
    return dict(residual=residual, chosen=chosen, footprint_tile=footprint_tile, footprint_block=footprint_block, interp=interp, speed=speed)


pseudo_rate = 0.16


def smooth_step(field, speed):
    padded = jnp.pad(field, 1)
    beside = padded[2:, 1:-1, 1:-1] + padded[:-2, 1:-1, 1:-1]
    beside = beside + padded[1:-1, 2:, 1:-1] + padded[1:-1, :-2, 1:-1]
    beside = beside + padded[1:-1, 1:-1, 2:] + padded[1:-1, 1:-1, :-2]
    return field + pseudo_rate * speed * (beside - 6.0 * field)


def reference(residual, chosen, footprint_tile, footprint_block, interp, speed):
    rows = residual.shape[0]
    keep = jnp.repeat(chosen, NBLK).astype(jnp.bfloat16)
    traces = residual * keep[:, None]
    injected = jnp.dot(traces.astype(jnp.float32), interp, precision=lax.Precision.HIGHEST)
    target = (footprint_tile * CBLK + footprint_block).reshape(-1).astype(jnp.int32)
    values = jnp.broadcast_to(injected[:, None, :], (rows, TOP, SAMP)).reshape(-1, SAMP)
    source = jax.ops.segment_sum(values, target, num_segments=N_TILE * CBLK)
    field = source.reshape(NX, NY, NZ)
    for step in range(STEPS):
        field = smooth_step(field, speed)
    blocks = field.reshape(-1, SAMP)
    sampled = jnp.dot(blocks[target], interp.T, precision=lax.Precision.HIGHEST)
    partials = jnp.sum(sampled.reshape(rows, TOP, SAMP), axis=1)
    return field, partials
```

```python
import functools

import jax
import jax.numpy as jnp
from jax import lax
from jax.experimental import pallas as pl
from jax.experimental.pallas import tpu as pltpu
from jax.sharding import PartitionSpec as P

CAP = 32
STEPS = 4
RATE = 0.16
HALO = STEPS - 1
CUTS = 2
MESH = pl.DeviceIdType.MESH
VMEM = pl.BlockSpec(memory_space=pltpu.VMEM)
ANY = pl.BlockSpec(memory_space=pl.ANY)
SMEM = pl.BlockSpec(memory_space=pltpu.SMEM)
F32 = jnp.float32
BF16 = jnp.bfloat16
HIGH = lax.Precision.HIGHEST


def iota(shape, dim):
    return lax.broadcasted_iota(jnp.int32, shape, dim)


def last_dims(a, b):
    return lax.dot_general(a, b, (((1,), (1,)), ((), ())), preferred_element_type=F32)


def dot32(a, b):
    return lax.dot_general(a, b, (((1,), (0,)), ((), ())), preferred_element_type=F32)


def pitch_of(geom):
    return geom[1] + 8


def plane_rows(geom):
    return 2 * geom[0] * pitch_of(geom) + 8


def outer_of(e, n):
    t = e - 1 if e % 2 == 0 else e + 1
    return t if 0 <= t < n else None


def thirds(x):
    a = x.astype(BF16)
    rest = x - a.astype(F32)
    b = rest.astype(BF16)
    return a, b, (rest - b.astype(F32)).astype(BF16)


def slot_rows(dest, tiles):
    top, rows = dest.shape
    upper = (iota((rows, rows), 0) < iota((rows, rows), 1)).astype(BF16)
    base = jnp.zeros((tiles, 1), F32)
    out = []
    for k in range(top):
        here = dest[k : k + 1, :]
        hot = (iota((tiles, rows), 0) == here).astype(F32)
        ahead = dot32(hot.astype(BF16), upper) + base
        rank = jnp.sum(hot * ahead, axis=0, keepdims=True).astype(jnp.int32)
        base = base + jnp.sum(hot, axis=1, keepdims=True)
        out.append((hot, rank, here * CAP + rank))
    return out


def pack(tiles, geom, res_ref, chosen_ref, ft_ref, fb_ref, pay, cod, place_ref):
    cx, ny, nz = geom
    nzb = nz // 128
    per_layer = ny * nzb
    top, rows = ft_ref.shape
    sensors = chosen_ref.shape[0]
    lane = iota((1, rows), 1)
    keep = jnp.zeros((1, rows), jnp.int32)
    for i in range(sensors):
        keep = jnp.where(lane // (rows // sensors) == i, chosen_ref[i], keep)
    keep = keep.astype(F32)
    block = fb_ref[...]
    dest = ft_ref[...]
    layer = jnp.zeros_like(block)
    for i in range(1, cx):
        layer = layer + (block >= i * per_layer).astype(jnp.int32)
    in_layer = block - layer * per_layer
    y = in_layer // nzb
    zb = in_layer - y * nzb
    turned = cx - 1 - layer
    odd = dest % 2 == 1
    within = zb * plane_rows(geom) + 8 + y
    flats = (
        within + (cx + jnp.where(odd, turned, layer)) * pitch_of(geom),
        within + jnp.where(odd, layer, turned) * pitch_of(geom),
    )
    slots = slot_rows(dest, tiles)
    place = jnp.zeros((tiles * CAP, rows), F32)
    codes = [jnp.zeros((tiles, 128), F32) for _ in flats]
    for k, (hot, rank, slot) in enumerate(slots):
        place = place + (iota((tiles * CAP, rows), 0) == slot).astype(F32)
        at = (iota((128, rows), 0) == rank).astype(BF16)
        for o, flat in enumerate(flats):
            hi = (flat // 64).astype(F32)
            lo = (flat - flat // 64 * 64).astype(F32)
            upper = last_dims((hot * hi[k : k + 1]).astype(BF16), at)
            lower = last_dims((hot * lo[k : k + 1]).astype(BF16), at)
            codes[o] = codes[o] + upper * 64.0 + lower
    place_ref[...] = place.astype(BF16)
    payload = dot32((place * keep).astype(BF16), res_ref[...]).astype(BF16)
    codes = [c.astype(jnp.int32) for c in codes]
    for e in range(tiles):
        t = outer_of(e, tiles)
        pay[e, 0] = payload[e * CAP : e * CAP + CAP]
        cod[e, 0] = codes[0][e : e + 1]
        pay[e, 1] = jnp.zeros((CAP, 128), BF16) if t is None else payload[t * CAP : t * CAP + CAP]
        cod[e, 1] = jnp.zeros((1, 128), jnp.int32) if t is None else codes[1][t : t + 1]


def signal_all(n, me, partner):
    barrier = pltpu.get_barrier_semaphore()

    @pl.loop(1, n)
    def _(i):
        pl.semaphore_signal(barrier, inc=1, device_id={"tile": lax.rem(me + i, n)}, device_id_type=MESH)

    if partner is not None:
        pl.semaphore_signal(barrier, inc=1, device_id={"group": partner}, device_id_type=MESH)


def wait_all(n, partner):
    pl.semaphore_wait(pltpu.get_barrier_semaphore(), n - 1 if partner is None else n)


def where_am_i(n, groups):
    me = lax.axis_index("tile")
    odd = lax.rem(me, 2)
    nb = me + 2 * odd - 1
    inter = jnp.logical_and(nb >= 0, nb < n)
    if groups % 2:
        return me, odd, nb, inter, None, 0
    g = lax.axis_index("group")
    half = lax.rem(g, 2)
    return me, odd, nb, inter, g + 1 - 2 * half, half


class Halo:
    def __init__(self, source, target, sems, forward_sems, nb, partner, half):
        layers, ny = target.shape[0], target.shape[1]
        self.count = layers * CUTS
        self.paired = partner is not None
        size = (ny // 2 if self.paired else ny) // CUTS
        start = half * (ny // 2) if self.paired else 0

        def window(i):
            return i // CUTS, pl.ds(start + i % CUTS * size, size)

        def piece(i):
            return pltpu.make_async_remote_copy(
                source.at[window(i)], target.at[window(i)], sems.at[0, i], sems.at[1, i],
                device_id={"tile": nb}, device_id_type=MESH)

        def forward(i):
            here = target.at[window(i)]
            return pltpu.make_async_remote_copy(
                here, here, forward_sems.at[0, i], forward_sems.at[1, i],
                device_id={"group": partner}, device_id_type=MESH)

        self.piece, self.forward = piece, forward

    def start(self, i):
        self.piece(i).start()

    def hand_on(self, i):
        self.piece(i).wait_recv()
        if self.paired:
            self.forward(i).start()

    def arrived(self, i):
        if self.paired:
            self.forward(i).wait_recv()

    def sent(self, i):
        self.piece(i).wait_send()
        if self.paired:
            self.forward(i).wait_send()


def exchange_kernel(
    n, groups, geom, res_ref, chosen_ref, ft_ref, fb_ref, interp, speed_in,
    vals, gotc, u, rate, halo, later, place_ref,
    first, pay, cod, got, ssem, sems, csems, isem, fsem, lsem
):
    cx, ny, nz = geom
    me, odd, nb, inter, partner, half = where_am_i(n, groups)
    signal_all(n, me, partner)
    loads = [
        pltpu.make_async_copy(speed_in.at[i + odd * (cx - 1 - 2 * i)], rate.at[i], ssem.at[i]) for i in range(cx)
    ]
    for load in loads:
        load.start()
    pack(n, geom, res_ref, chosen_ref, ft_ref, fb_ref, pay, cod, place_ref)

    def scale(i):
        @pl.loop(0, ny // 16)
        def _(r):
            rows = pl.ds(pl.multiple_of(r * 16, 16), 16)
            new = RATE * rate[i, rows]
            rate[i, rows] = new
            if i == 0:
                first[0, rows] = new.astype(BF16)
            elif i < HALO:
                later[i - 1, rows] = new.astype(BF16)

    loads[0].wait()
    scale(0)
    wait_all(n, partner)

    def data(i):
        e = lax.rem(me + i, n)
        return pltpu.make_async_remote_copy(
            pay.at[e], got.at[me], sems.at[0, i], sems.at[1, i],
            device_id={"tile": e}, device_id_type=MESH)

    def code(i):
        e = lax.rem(me + i, n)
        return pltpu.make_async_remote_copy(
            cod.at[e], gotc.at[me], csems.at[0, i], csems.at[1, i],
            device_id={"tile": e}, device_id_type=MESH)

    beside = Halo(first, halo, isem, fsem, nb, partner, half)

    @pl.when(inter)
    def _():
        for i in range(beside.count):
            beside.start(i)

    @pl.loop(1, n)
    def _(i):
        data(i).start()
        code(i).start()

    own = pltpu.make_async_copy(pay.at[me], got.at[me], lsem.at[0])
    ownc = pltpu.make_async_copy(cod.at[me], gotc.at[me], lsem.at[1])
    own.start()
    ownc.start()

    zero = jnp.zeros((8, 128), F32)
    flat = u.shape[0]

    @pl.loop(0, flat // 128)
    def _(s):
        for i in range(16):
            u[pl.ds(pl.multiple_of(s * 128 + i * 8, 8), 8)] = zero

    for row in range(flat // 128 * 128, flat, 8):
        u[row : row + 8] = zero
    for i in range(1, cx):
        loads[i].wait()
        scale(i)

    @pl.when(inter)
    def _():
        for i in range(beside.count):
            beside.hand_on(i)

    @pl.when(jnp.logical_not(inter))
    def _():
        halo[...] = jnp.zeros(halo.shape, halo.dtype)

    parts = jnp.concatenate(thirds(interp[...]), axis=1)

    def inject(s):
        three = dot32(got[s].reshape(2 * CAP, 128), parts)
        vals[s] = three[:, :128] + (three[:, 128:256] + three[:, 256:])

    own.wait()
    inject(me)

    @pl.loop(1, n)
    def _(i):
        data(i).wait()
        inject(lax.rem(me - i + n, n))

    @pl.loop(1, n)
    def _(i):
        code(i).wait()

    ownc.wait()

    @pl.when(inter)
    def _():
        for i in range(beside.count):
            beside.arrived(i)
            beside.sent(i)


def inject_kernel(codes, vals, u_in, u):
    @pl.loop(0, vals.shape[0])
    def _(s):
        for j in range(CAP):
            own, outer = codes[s * 2, j], codes[s * 2 + 1, j]
            a, b = u[pl.ds(own, 1)], u[pl.ds(outer, 1)]
            u[pl.ds(own, 1)] = a + vals[s, pl.ds(j, 1)]
            u[pl.ds(outer, 1)] = b + vals[s, pl.ds(CAP + j, 1)]


def step_kernel(
    n, groups, geom, u0, codes, rate, halo, later, u4, ret,
    u1, u2, u3, edge, deep, sampled, isem, fsem, esem, sems, lsem
):
    cx, ny, nz = geom
    nzb = nz // 128
    pitch = pitch_of(geom)
    plane = plane_rows(geom)
    me, odd, nb, inter, partner, half = where_am_i(n, groups)
    signal_all(n, me, partner)
    zero = jnp.zeros((8, 128), F32)
    for ref in (u1, u2, u3):
        for zb in range(nzb):
            for m in range(2 * cx + 1):
                ref[zb, m * pitch : m * pitch + 8] = zero
    u4[0:8] = zero

    @pl.when(jnp.logical_not(inter))
    def _():
        deep[...] = jnp.zeros(deep.shape, deep.dtype)

    wait_all(n, partner)
    last = 2 * cx - 1
    beside = Halo(later, deep, isem, fsem, nb, partner, half)

    def swap(src, step):
        return pltpu.make_async_remote_copy(
            src.at[:, pl.ds(last * pitch + 8, ny)], edge.at[step], esem.at[0, step], esem.at[1, step],
            device_id={"tile": me + 1 - 2 * odd}, device_id_type=MESH)

    swap(u0, 0).start()

    @pl.when(inter)
    def _():
        for i in range(beside.count):
            beside.start(i)

    lane = iota((8, 128), 1)
    first_lane, last_lane = lane == 0, lane == 127

    def step_rows(step, src, dst, lo, hi, row):
        rates = {}
        for h in range(2):
            at = pl.multiple_of(row + h * 8, 8)
            base = at + 8

            def strip(m):
                if m > last:
                    return [edge[step, zb, pl.ds(at, 8)] for zb in range(nzb)]
                return [src[zb, pl.ds(base + m * pitch, 8)] for zb in range(nzb)]

            below, here = strip(lo - 1), strip(lo)
            for m in range(lo, hi):
                above = strip(m + 1)
                for zb in range(nzb):
                    lanes = slice(zb * 128, zb * 128 + 128)
                    if m >= cx:
                        r = rate[m - cx, pl.ds(at, 8), lanes]
                    else:
                        if h == 0:
                            got = halo[0, pl.ds(row, 16), lanes] if m == cx - 1 else deep[cx - 2 - m, pl.ds(row, 16), lanes]
                            rates[m, zb] = got.astype(F32)
                        r = rates[m, zb][h * 8 : h * 8 + 8]
                    c = here[zb]
                    left = here[zb - 1] if zb > 0 else 0.0
                    right = here[zb + 1] if zb + 1 < nzb else 0.0
                    total = below[zb] + above[zb]
                    total = total + (src[zb, pl.ds(base + m * pitch - 1, 8)] + src[zb, pl.ds(base + m * pitch + 1, 8)])
                    total = total + pltpu.roll(jnp.where(last_lane, left, c), 1, 1)
                    total = total + pltpu.roll(jnp.where(first_lane, right, c), 127, 1)
                    new = c + r * (total - 6.0 * c)
                    if dst is u4:
                        dst[pl.ds(zb * plane + base + m * pitch, 8)] = new
                    else:
                        dst[zb, pl.ds(base + m * pitch, 8)] = new
                below, here = here, above

    fields = (u0, u1, u2, u3, u4)

    def step(k, lo, hi):
        rows = 16 if hi - lo > 2 else 32

        @pl.loop(0, ny // rows)
        def _(p):
            for q in range(0, rows, 16):
                step_rows(k, fields[k], fields[k + 1], lo, hi, pl.multiple_of(p * rows + q, 16))

    def close(k):
        swap(fields[k], k).wait_recv()
        step(k, last, last + 1)
        if k < STEPS - 1:
            swap(fields[k + 1], k + 1).start()

    def on_halo(act, layer):
        @pl.when(inter)
        def _():
            for i in range(layer * CUTS, layer * CUTS + CUTS):
                act(i)

    step(0, cx - 1, last)
    close(0)
    on_halo(beside.hand_on, 0)
    step(1, cx, last)
    close(1)
    on_halo(beside.arrived, 0)
    step(0, cx - 2, cx - 1)
    step(1, cx - 1, cx)
    on_halo(beside.hand_on, 1)
    step(2, cx, last)
    close(2)
    on_halo(beside.arrived, 1)
    step(0, cx - 3, cx - 2)
    step(1, cx - 2, cx - 1)
    step(2, cx - 1, cx)
    step(3, cx, last)
    close(3)

    def block(i):
        e = lax.rem(me + i, n)
        return pltpu.make_async_remote_copy(
            sampled.at[e], ret.at[me], sems.at[0, i], sems.at[1, i],
            device_id={"tile": e}, device_id_type=MESH)

    def sample(e):
        for j in range(CAP):
            sampled[e, pl.ds(j, 1)] = u4[pl.ds(codes[e * 2, j], 1)]

    @pl.loop(1, n)
    def _(i):
        sample(lax.rem(me + i, n))
        block(i).start()

    sample(me)
    own = pltpu.make_async_copy(sampled.at[me], ret.at[me], lsem)
    own.start()
    on_halo(beside.sent, 0)
    on_halo(beside.sent, 1)
    for k in range(STEPS):
        swap(fields[k], k).wait_send()
    own.wait()

    @pl.loop(1, n)
    def _(i):
        block(i).wait()


def finish_kernel(geom, u4, ret, place, interp, field, out, sems):
    cx, ny, nz = geom
    pitch = pitch_of(geom)
    plane = plane_rows(geom)
    odd = lax.rem(lax.axis_index("tile"), 2)
    copies = [
        pltpu.make_async_copy(
            u4.at[pl.ds(zb * plane + (cx + i) * pitch + 8, ny)],
            field.at[i + odd * (cx - 1 - 2 * i), :, pl.ds(zb * 128, 128)],
            sems.at[i, zb])
        for i in range(cx) for zb in range(nz // 128)
    ]
    for copy in copies:
        copy.start()
    parts = jnp.concatenate(thirds(ret[...].reshape(-1, 128)), axis=1)
    three = lax.dot_general(place[...], parts, (((0,), (0,)), ((), ())), preferred_element_type=F32)
    total = three[:, :128] + (three[:, 128:256] + three[:, 256:])
    out[...] = lax.dot_general(
        total, interp[...], (((1,), (1,)), ((), ())), precision=HIGH, preferred_element_type=F32)
    for copy in copies:
        copy.wait()


def params(mib, **more):
    return pltpu.CompilerParams(vmem_limit_bytes=mib * 2**20, **more)


def body(groups, residual, chosen, footprint_tile, footprint_block, interp, speed):
    n = lax.axis_size("tile")
    cx, ny, nz = geom = speed.shape
    rows, samp = residual.shape
    nzb = nz // 128
    shape = jax.ShapeDtypeStruct
    dma = pltpu.SemaphoreType.DMA
    plane = plane_rows(geom)
    vals, codes, u0, rate, halo, later, place = pl.pallas_call(
        functools.partial(exchange_kernel, n, groups, geom),
        out_shape=(
            shape((n, 2 * CAP, samp), F32),
            shape((n, 2, 1, 128), jnp.int32),
            shape((nzb * plane, 128), F32),
            shape(geom, F32),
            shape((1, ny, nz), BF16),
            shape((HALO - 1, ny, nz), BF16),
            shape((n * CAP, rows), BF16),
        ),
        in_specs=[VMEM, SMEM, VMEM, VMEM, VMEM, ANY],
        out_specs=(VMEM,) * 7,
        scratch_shapes=[
            pltpu.VMEM((1, ny, nz), BF16),
            pltpu.VMEM((n, 2, CAP, samp), BF16), pltpu.VMEM((n, 2, 1, 128), jnp.int32),
            pltpu.VMEM((n, 2, CAP, samp), BF16),
            dma((cx,)), dma((2, n)), dma((2, n)), dma((2, CUTS)), dma((2, CUTS)), dma((2,)),
        ],
        compiler_params=params(10, collective_id=0, has_side_effects=True),
        name="exchange",
    )(residual, chosen, footprint_tile.T, footprint_block.T, interp, speed)
    codes = codes.reshape(n * 2, 128)
    u0 = pl.pallas_call(
        inject_kernel,
        out_shape=shape(u0.shape, F32),
        in_specs=[SMEM, VMEM, VMEM],
        out_specs=VMEM,
        input_output_aliases={2: 0},
        compiler_params=params(4),
        name="inject",
    )(codes, vals, u0)
    layers = pltpu.VMEM((nzb, plane, 128), F32)
    u4, ret = pl.pallas_call(
        functools.partial(step_kernel, n, groups, geom),
        out_shape=(shape((nzb * plane, 128), F32), shape((n, CAP, samp), F32)),
        in_specs=[VMEM, SMEM, VMEM, VMEM, VMEM],
        out_specs=(VMEM,) * 2,
        scratch_shapes=[
            layers, layers, layers,
            pltpu.VMEM((STEPS, nzb, ny, 128), F32), pltpu.VMEM((HALO - 1, ny, nz), BF16),
            pltpu.VMEM((n, CAP, samp), F32),
            dma((2, (HALO - 1) * CUTS)), dma((2, (HALO - 1) * CUTS)), dma((2, STEPS)), dma((2, n)), dma,
        ],
        compiler_params=params(30, collective_id=1, has_side_effects=True),
        name="steps",
    )(u0.reshape(nzb, plane, 128), codes, rate, halo, later)
    return pl.pallas_call(
        functools.partial(finish_kernel, geom),
        out_shape=(shape(geom, F32), shape((rows, samp), F32)),
        in_specs=[VMEM] * 4,
        out_specs=(ANY, VMEM),
        scratch_shapes=[dma((cx, nzb))],
        compiler_params=params(8),
        name="finish",
    )(u4, ret, place, interp)


def solution(mesh):
    placed = (
        P(("group", "tile"), None),
        P(("group", "tile")),
        P("tile", None),
        P("tile", None),
        P(),
        P("tile", None, None),
    )
    return jax.shard_map(
        functools.partial(body, mesh.shape["group"]),
        mesh=mesh,
        in_specs=placed,
        out_specs=(P(("group", "tile"), None, None), P(("group", "tile"), None)),
        check_vma=False,
    )
```

```python
import functools

import jax
import jax.numpy as jnp
from jax import lax
from jax.experimental import pallas as pl
from jax.experimental.pallas import tpu as pltpu
from jax.sharding import PartitionSpec as P

CAP = 32
STEPS = 4
RATE = 0.16
HALO = STEPS - 1
CUTS = 2
EARLY = 2
BODY = 16
BATCH = 8
MESH = pl.DeviceIdType.MESH
VMEM = pl.BlockSpec(memory_space=pltpu.VMEM)
HBM = pl.BlockSpec(memory_space=pltpu.HBM)
ANY = pl.BlockSpec(memory_space=pl.ANY)
SMEM = pl.BlockSpec(memory_space=pltpu.SMEM)
F32 = jnp.float32
BF16 = jnp.bfloat16
HIGH = lax.Precision.HIGHEST


def iota(shape, dim):
    return lax.broadcasted_iota(jnp.int32, shape, dim)


def last_dims(a, b):
    return lax.dot_general(a, b, (((1,), (1,)), ((), ())), preferred_element_type=F32)


def dot32(a, b):
    return lax.dot_general(a, b, (((1,), (0,)), ((), ())), preferred_element_type=F32)


def pitch_of(geom):
    return geom[1] + 8


def plane_rows(geom):
    return 2 * geom[0] * pitch_of(geom) + 8


def outer_of(e, n):
    t = e - 1 if e % 2 == 0 else e + 1
    return t if 0 <= t < n else None


def thirds(x):
    a = x.astype(BF16)
    rest = x - a.astype(F32)
    b = rest.astype(BF16)
    return a, b, (rest - b.astype(F32)).astype(BF16)


def slot_rows(dest, tiles):
    top, rows = dest.shape
    upper = (iota((rows, rows), 0) < iota((rows, rows), 1)).astype(BF16)
    base = jnp.zeros((tiles, 1), F32)
    out = []
    for k in range(top):
        here = dest[k : k + 1, :]
        hot = (iota((tiles, rows), 0) == here).astype(F32)
        ahead = dot32(hot.astype(BF16), upper) + base
        rank = jnp.sum(hot * ahead, axis=0, keepdims=True).astype(jnp.int32)
        base = base + jnp.sum(hot, axis=1, keepdims=True)
        out.append((hot, rank, here * CAP + rank))
    return out


def pack(tiles, geom, res_ref, chosen_ref, ft_ref, fb_ref, pay, cod, place_ref):
    cx, ny, nz = geom
    nzb = nz // 128
    per_layer = ny * nzb
    top, rows = ft_ref.shape
    sensors = chosen_ref.shape[0]
    lane = iota((1, rows), 1)
    keep = jnp.zeros((1, rows), jnp.int32)
    for i in range(sensors):
        keep = jnp.where(lane // (rows // sensors) == i, chosen_ref[i], keep)
    keep = keep.astype(F32)
    block = fb_ref[...]
    dest = ft_ref[...]
    layer = jnp.zeros_like(block)
    for i in range(1, cx):
        layer = layer + (block >= i * per_layer).astype(jnp.int32)
    in_layer = block - layer * per_layer
    y = in_layer // nzb
    zb = in_layer - y * nzb
    turned = cx - 1 - layer
    odd = dest % 2 == 1
    within = zb * plane_rows(geom) + 8 + y
    flats = (
        within + (cx + jnp.where(odd, turned, layer)) * pitch_of(geom),
        within + jnp.where(odd, layer, turned) * pitch_of(geom),
    )
    slots = slot_rows(dest, tiles)
    place = jnp.zeros((tiles * CAP, rows), F32)
    codes = [jnp.zeros((tiles, 128), F32) for _ in flats]
    for k, (hot, rank, slot) in enumerate(slots):
        place = place + (iota((tiles * CAP, rows), 0) == slot).astype(F32)
        at = (iota((128, rows), 0) == rank).astype(BF16)
        for o, flat in enumerate(flats):
            hi = (flat // 64).astype(F32)
            lo = (flat - flat // 64 * 64).astype(F32)
            upper = last_dims((hot * hi[k : k + 1]).astype(BF16), at)
            lower = last_dims((hot * lo[k : k + 1]).astype(BF16), at)
            codes[o] = codes[o] + upper * 64.0 + lower
    place_ref[...] = place.astype(BF16)
    payload = dot32((place * keep).astype(BF16), res_ref[...]).astype(BF16)
    codes = [c.astype(jnp.int32) for c in codes]
    for e in range(tiles):
        t = outer_of(e, tiles)
        pay[e, 0] = payload[e * CAP : e * CAP + CAP]
        cod[e, 0] = codes[0][e : e + 1]
        pay[e, 1] = jnp.zeros((CAP, 128), BF16) if t is None else payload[t * CAP : t * CAP + CAP]
        cod[e, 1] = jnp.zeros((1, 128), jnp.int32) if t is None else codes[1][t : t + 1]


def signal_all(n, me, partner):
    barrier = pltpu.get_barrier_semaphore()

    @pl.loop(1, n)
    def _(i):
        pl.semaphore_signal(barrier, inc=1, device_id={"tile": lax.rem(me + i, n)}, device_id_type=MESH)

    if partner is not None:
        pl.semaphore_signal(barrier, inc=1, device_id={"group": partner}, device_id_type=MESH)


def wait_all(n, partner):
    pl.semaphore_wait(pltpu.get_barrier_semaphore(), n - 1 if partner is None else n)


def where_am_i(n, groups):
    me = lax.axis_index("tile")
    odd = lax.rem(me, 2)
    nb = me + 2 * odd - 1
    inter = jnp.logical_and(nb >= 0, nb < n)
    if groups % 2:
        return me, odd, nb, inter, None, 0
    g = lax.axis_index("group")
    half = lax.rem(g, 2)
    return me, odd, nb, inter, g + 1 - 2 * half, half


class Halo:
    def __init__(self, source, target, sems, forward_sems, nb, partner, half):
        layers, ny = target.shape[0], target.shape[1]
        self.count = layers * CUTS
        self.paired = partner is not None
        size = (ny // 2 if self.paired else ny) // CUTS
        start = half * (ny // 2) if self.paired else 0

        def window(i):
            return i // CUTS, pl.ds(start + i % CUTS * size, size)

        def piece(i):
            return pltpu.make_async_remote_copy(
                source.at[window(i)], target.at[window(i)], sems.at[0, i], sems.at[1, i],
                device_id={"tile": nb}, device_id_type=MESH)

        def forward(i):
            here = target.at[window(i)]
            return pltpu.make_async_remote_copy(
                here, here, forward_sems.at[0, i], forward_sems.at[1, i],
                device_id={"group": partner}, device_id_type=MESH)

        self.piece, self.forward = piece, forward

    def start(self, i):
        self.piece(i).start()

    def hand_on(self, i):
        self.piece(i).wait_recv()
        if self.paired:
            self.forward(i).start()

    def arrived(self, i):
        if self.paired:
            self.forward(i).wait_recv()

    def sent(self, i):
        self.piece(i).wait_send()
        if self.paired:
            self.forward(i).wait_send()


def exchange_kernel(
    n, groups, geom, res_in, chosen_in, ft_in, fb_in, interp_in, speed_in,
    vals, gotc, u, rate, halo, later, place_ref,
    res_ref, chosen_ref, ft_ref, fb_ref, interp, first, pay, cod, got, nsem, ssem, sems, csems, isem, fsem, lsem
):
    cx, ny, nz = geom
    me, odd, nb, inter, partner, half = where_am_i(n, groups)
    signal_all(n, me, partner)
    loads = [
        pltpu.make_async_copy(speed_in.at[i + odd * (cx - 1 - 2 * i)], rate.at[i], ssem.at[i]) for i in range(cx)
    ]
    small = [
        pltpu.make_async_copy(a, b, nsem.at[i])
        for i, (a, b) in enumerate((
            (ft_in, ft_ref), (fb_in, fb_ref), (chosen_in, chosen_ref), (res_in, res_ref), (interp_in, interp)))
    ]
    for load in small + loads:
        load.start()
    for load in small:
        load.wait()
    pack(n, geom, res_ref, chosen_ref, ft_ref, fb_ref, pay, cod, place_ref)

    def scale(i):
        @pl.loop(0, ny // 16)
        def _(r):
            rows = pl.ds(pl.multiple_of(r * 16, 16), 16)
            new = RATE * rate[i, rows]
            rate[i, rows] = new
            if i < EARLY:
                first[i, rows] = new.astype(BF16)
            elif i < HALO:
                later[i - EARLY, rows] = new.astype(BF16)

    for i in range(EARLY):
        loads[i].wait()
        scale(i)
    wait_all(n, partner)

    def data(i):
        e = lax.rem(me + i, n)
        return pltpu.make_async_remote_copy(
            pay.at[e], got.at[me], sems.at[0, i], sems.at[1, i],
            device_id={"tile": e}, device_id_type=MESH)

    def code(i):
        e = lax.rem(me + i, n)
        return pltpu.make_async_remote_copy(
            cod.at[e], gotc.at[me], csems.at[0, i], csems.at[1, i],
            device_id={"tile": e}, device_id_type=MESH)

    beside = Halo(first, halo, isem, fsem, nb, partner, half)

    @pl.when(inter)
    def _():
        for i in range(beside.count):
            beside.start(i)

    @pl.loop(1, n)
    def _(i):
        data(i).start()
        code(i).start()

    own = pltpu.make_async_copy(pay.at[me], got.at[me], lsem.at[0])
    ownc = pltpu.make_async_copy(cod.at[me], gotc.at[me], lsem.at[1])
    own.start()
    ownc.start()

    zero = jnp.zeros((8, 128), F32)
    flat = u.shape[0]

    @pl.loop(0, flat // 128)
    def _(s):
        for i in range(16):
            u[pl.ds(pl.multiple_of(s * 128 + i * 8, 8), 8)] = zero

    for row in range(flat // 128 * 128, flat, 8):
        u[row : row + 8] = zero
    for i in range(EARLY, cx):
        loads[i].wait()
        scale(i)

    @pl.when(inter)
    def _():
        for i in range(beside.count):
            beside.hand_on(i)

    @pl.when(jnp.logical_not(inter))
    def _():
        halo[...] = jnp.zeros(halo.shape, halo.dtype)

    parts = jnp.concatenate(thirds(interp[...]), axis=1)

    size = 2 * CAP
    left, right = iota((size, size), 0), iota((size, size), 1)
    same, batch = left == right, left // BATCH == right // BATCH

    def inject(s):
        three = dot32(got[s].reshape(size, 128), parts)
        three = three[:, :128] + (three[:, 128:256] + three[:, 256:])
        across = jnp.concatenate([gotc[s, 0][:, :CAP], gotc[s, 1][:, :CAP]], axis=1)
        down = jnp.sum(jnp.where(same, across.astype(F32), 0.0), axis=1, keepdims=True)
        merge = jnp.logical_and(batch, down == across.astype(F32)).astype(BF16)
        three = dot32(merge, jnp.concatenate(thirds(three), axis=1))
        vals[s] = three[:, :128] + (three[:, 128:256] + three[:, 256:])

    own.wait()
    ownc.wait()
    inject(me)

    @pl.loop(1, n)
    def _(i):
        data(i).wait()
        code(i).wait()
        inject(lax.rem(me - i + n, n))

    @pl.when(inter)
    def _():
        for i in range(beside.count):
            beside.arrived(i)
            beside.sent(i)


def inject_kernel(codes, vals, u_in, u):
    @pl.loop(0, vals.shape[0])
    def _(s):
        for group in range(0, CAP, BATCH):
            rows = [(o, j) for j in range(group, group + BATCH) for o in range(2)]
            ats = [codes[s * 2 + o, j] for o, j in rows]
            new = [u[pl.ds(at, 1)] + vals[s, pl.ds(o * CAP + j, 1)] for at, (o, j) in zip(ats, rows)]
            for at, row in zip(ats, new):
                u[pl.ds(at, 1)] = row


def step_kernel(
    n, groups, geom, u0, codes, rate, halo, later, u4, ret,
    u1, u2, u3, edge, deep, sampled, isem, fsem, esem, sems, lsem
):
    cx, ny, nz = geom
    nzb = nz // 128
    pitch = pitch_of(geom)
    plane = plane_rows(geom)
    me, odd, nb, inter, partner, half = where_am_i(n, groups)
    signal_all(n, me, partner)
    zero = jnp.zeros((8, 128), F32)
    for ref in (u1, u2, u3):
        for zb in range(nzb):
            for m in range(2 * cx + 1):
                ref[zb, m * pitch : m * pitch + 8] = zero
    u4[0:8] = zero

    @pl.when(jnp.logical_not(inter))
    def _():
        deep[...] = jnp.zeros(deep.shape, deep.dtype)

    wait_all(n, partner)
    last = 2 * cx - 1
    beside = Halo(later, deep, isem, fsem, nb, partner, half)

    def swap(src, step):
        return pltpu.make_async_remote_copy(
            src.at[:, pl.ds(last * pitch + 8, ny)], edge.at[step], esem.at[0, step], esem.at[1, step],
            device_id={"tile": me + 1 - 2 * odd}, device_id_type=MESH)

    swap(u0, 0).start()

    @pl.when(inter)
    def _():
        for i in range(beside.count):
            beside.start(i)

    lane = iota((BODY, 128), 1)
    first_lane, last_lane = lane == 0, lane == 127

    def step_rows(step, src, dst, lo, hi, row):
        base = row + 8

        def strip(m):
            if m > last:
                return [edge[step, zb, pl.ds(row, BODY)] for zb in range(nzb)]
            return [src[zb, pl.ds(base + m * pitch, BODY)] for zb in range(nzb)]

        below, here = strip(lo - 1), strip(lo)
        for m in range(lo, hi):
            above = strip(m + 1)
            for zb in range(nzb):
                lanes = slice(zb * 128, zb * 128 + 128)
                if m >= cx:
                    r = rate[m - cx, pl.ds(row, BODY), lanes]
                elif cx - 1 - m < EARLY:
                    r = halo[cx - 1 - m, pl.ds(row, BODY), lanes].astype(F32)
                else:
                    r = deep[cx - 1 - m - EARLY, pl.ds(row, BODY), lanes].astype(F32)
                c = here[zb]
                left = here[zb - 1] if zb > 0 else 0.0
                right = here[zb + 1] if zb + 1 < nzb else 0.0
                total = below[zb] + above[zb]
                total = total + (
                    src[zb, pl.ds(base + m * pitch - 1, BODY)] + src[zb, pl.ds(base + m * pitch + 1, BODY)])
                total = total + pltpu.roll(jnp.where(last_lane, left, c), 1, 1)
                total = total + pltpu.roll(jnp.where(first_lane, right, c), 127, 1)
                new = c + r * (total - 6.0 * c)
                if dst is u4:
                    dst[pl.ds(zb * plane + base + m * pitch, BODY)] = new
                else:
                    dst[zb, pl.ds(base + m * pitch, BODY)] = new
            below, here = here, above

    fields = (u0, u1, u2, u3, u4)

    def step(k, lo, hi):
        rows = ny // 2 if hi - lo > 1 else ny

        def part(start):
            for q in range(0, rows, BODY):
                step_rows(k, fields[k], fields[k + 1], lo, hi, start + q)

        if rows == ny:
            part(0)
        else:
            pl.loop(0, 2)(lambda p: part(pl.multiple_of(p * rows, BODY)))

    def close(k):
        swap(fields[k], k).wait_recv()
        step(k, last, last + 1)
        if k < STEPS - 1:
            swap(fields[k + 1], k + 1).start()

    def on_halo(act, layer):
        @pl.when(inter)
        def _():
            for i in range(layer * CUTS, layer * CUTS + CUTS):
                act(i)

    def halo_layer(act, d):
        if d > EARLY:
            on_halo(act, d - 1 - EARLY)

    step(0, cx - 1, last)
    close(0)
    halo_layer(beside.hand_on, 2)
    halo_layer(beside.arrived, 2)
    step(0, cx - 2, cx - 1)
    step(1, cx - 1, cx)
    step(1, cx, last)
    close(1)
    halo_layer(beside.hand_on, 3)
    step(2, cx, last)
    halo_layer(beside.arrived, 3)
    step(0, cx - 3, cx - 2)
    step(1, cx - 2, cx - 1)
    close(2)
    step(2, cx - 1, cx)
    step(3, cx, last)
    close(3)

    def block(i):
        e = lax.rem(me + i, n)
        return pltpu.make_async_remote_copy(
            sampled.at[e], ret.at[me], sems.at[0, i], sems.at[1, i],
            device_id={"tile": e}, device_id_type=MESH)

    def sample(e):
        for j in range(CAP):
            sampled[e, pl.ds(j, 1)] = u4[pl.ds(codes[e * 2, j], 1)]

    @pl.loop(1, n)
    def _(i):
        sample(lax.rem(me + i, n))
        block(i).start()

    sample(me)
    own = pltpu.make_async_copy(sampled.at[me], ret.at[me], lsem)
    own.start()
    halo_layer(beside.sent, 2)
    halo_layer(beside.sent, 3)
    for k in range(STEPS):
        swap(fields[k], k).wait_send()
    own.wait()

    @pl.loop(1, n)
    def _(i):
        block(i).wait()


def finish_kernel(geom, u4, ret, place, interp, field, out, sems):
    cx, ny, nz = geom
    pitch = pitch_of(geom)
    plane = plane_rows(geom)
    odd = lax.rem(lax.axis_index("tile"), 2)
    copies = [
        pltpu.make_async_copy(
            u4.at[pl.ds(zb * plane + (cx + i) * pitch + 8, ny)],
            field.at[i + odd * (cx - 1 - 2 * i), :, pl.ds(zb * 128, 128)],
            sems.at[i, zb])
        for i in range(cx) for zb in range(nz // 128)
    ]
    for copy in copies:
        copy.start()
    parts = jnp.concatenate(thirds(ret[...].reshape(-1, 128)), axis=1)
    three = lax.dot_general(place[...], parts, (((0,), (0,)), ((), ())), preferred_element_type=F32)
    total = three[:, :128] + (three[:, 128:256] + three[:, 256:])
    out[...] = lax.dot_general(
        total, interp[...], (((1,), (1,)), ((), ())), precision=HIGH, preferred_element_type=F32)
    for copy in copies:
        copy.wait()


def in_hbm(x):
    return pltpu.with_memory_space_constraint(x, pltpu.HBM)


def params(mib, **more):
    return pltpu.CompilerParams(vmem_limit_bytes=mib * 2**20, **more)


def body(groups, residual, chosen, footprint_tile, footprint_block, interp, speed):
    n = lax.axis_size("tile")
    cx, ny, nz = geom = speed.shape
    rows, samp = residual.shape
    nzb = nz // 128
    shape = jax.ShapeDtypeStruct
    dma = pltpu.SemaphoreType.DMA
    plane = plane_rows(geom)
    vals, codes, u0, rate, halo, later, place = pl.pallas_call(
        functools.partial(exchange_kernel, n, groups, geom),
        out_shape=(
            shape((n, 2 * CAP, samp), F32),
            shape((n, 2, 1, 128), jnp.int32),
            shape((nzb * plane, 128), F32),
            shape(geom, F32),
            shape((EARLY, ny, nz), BF16),
            shape((HALO - EARLY, ny, nz), BF16),
            shape((n * CAP, rows), BF16),
        ),
        in_specs=[HBM] * 6,
        out_specs=(VMEM,) * 7,
        scratch_shapes=[
            pltpu.VMEM((rows, samp), BF16), pltpu.SMEM(chosen.shape, jnp.int32),
            pltpu.VMEM(footprint_tile.shape[::-1], jnp.int32), pltpu.VMEM(footprint_tile.shape[::-1], jnp.int32),
            pltpu.VMEM((samp, samp), F32),
            pltpu.VMEM((EARLY, ny, nz), BF16),
            pltpu.VMEM((n, 2, CAP, samp), BF16), pltpu.VMEM((n, 2, 1, 128), jnp.int32),
            pltpu.VMEM((n, 2, CAP, samp), BF16),
            dma((5,)), dma((cx,)), dma((2, n)), dma((2, n)), dma((2, EARLY * CUTS)), dma((2, EARLY * CUTS)), dma((2,)),
        ],
        compiler_params=params(10, collective_id=0, has_side_effects=True),
        name="exchange",
    )(*(in_hbm(x) for x in (residual, chosen, footprint_tile.T, footprint_block.T, interp, speed)))
    codes = codes.reshape(n * 2, 128)
    u0 = pl.pallas_call(
        inject_kernel,
        out_shape=shape(u0.shape, F32),
        in_specs=[SMEM, VMEM, VMEM],
        out_specs=VMEM,
        input_output_aliases={2: 0},
        compiler_params=params(4),
        name="inject",
    )(codes, vals, u0)
    layers = pltpu.VMEM((nzb, plane, 128), F32)
    u4, ret = pl.pallas_call(
        functools.partial(step_kernel, n, groups, geom),
        out_shape=(shape((nzb * plane, 128), F32), shape((n, CAP, samp), F32)),
        in_specs=[VMEM, SMEM, VMEM, VMEM, VMEM],
        out_specs=(VMEM,) * 2,
        scratch_shapes=[
            layers, layers, layers,
            pltpu.VMEM((STEPS, nzb, ny, 128), F32), pltpu.VMEM((HALO - EARLY, ny, nz), BF16),
            pltpu.VMEM((n, CAP, samp), F32),
            dma((2, (HALO - EARLY) * CUTS)), dma((2, (HALO - EARLY) * CUTS)), dma((2, STEPS)), dma((2, n)), dma,
        ],
        compiler_params=params(30, collective_id=1, has_side_effects=True),
        name="steps",
    )(u0.reshape(nzb, plane, 128), codes, rate, halo, later)
    return pl.pallas_call(
        functools.partial(finish_kernel, geom),
        out_shape=(shape(geom, F32), shape((rows, samp), F32)),
        in_specs=[VMEM] * 4,
        out_specs=(ANY, VMEM),
        scratch_shapes=[dma((cx, nzb))],
        compiler_params=params(8),
        name="finish",
    )(u4, ret, place, interp)


def solution(mesh):
    placed = (
        P(("group", "tile"), None),
        P(("group", "tile")),
        P("tile", None),
        P("tile", None),
        P(),
        P("tile", None, None),
    )
    return jax.shard_map(
        functools.partial(body, mesh.shape["group"]),
        mesh=mesh,
        in_specs=placed,
        out_specs=(P(("group", "tile"), None, None), P(("group", "tile"), None)),
        check_vma=False,
    )
```

```python
import functools

import jax
import jax.numpy as jnp
from jax import lax
from jax.experimental import pallas as pl
from jax.experimental.pallas import tpu as pltpu
from jax.sharding import PartitionSpec as P

CAP = 32
STEPS = 4
RATE = 0.16
HALO = STEPS - 1
CUTS = 2
EARLY = 1
BODY = 16
BATCH = 8
LEVELS = 32767.0
MESH = pl.DeviceIdType.MESH
VMEM = pl.BlockSpec(memory_space=pltpu.VMEM)
HBM = pl.BlockSpec(memory_space=pltpu.HBM)
ANY = pl.BlockSpec(memory_space=pl.ANY)
SMEM = pl.BlockSpec(memory_space=pltpu.SMEM)
F32 = jnp.float32
BF16 = jnp.bfloat16
HIGH = lax.Precision.HIGHEST


def iota(shape, dim):
    return lax.broadcasted_iota(jnp.int32, shape, dim)


def last_dims(a, b):
    return lax.dot_general(a, b, (((1,), (1,)), ((), ())), preferred_element_type=F32)


def dot32(a, b):
    return lax.dot_general(a, b, (((1,), (0,)), ((), ())), preferred_element_type=F32)


def pitch_of(geom):
    return geom[1] + 8


def plane_rows(geom):
    return 2 * geom[0] * pitch_of(geom) + 8


def outer_of(e, n):
    t = e - 1 if e % 2 == 0 else e + 1
    return t if 0 <= t < n else None


def thirds(x):
    a = x.astype(BF16)
    rest = x - a.astype(F32)
    b = rest.astype(BF16)
    return a, b, (rest - b.astype(F32)).astype(BF16)


def slot_rows(dest, tiles):
    top, rows = dest.shape
    upper = (iota((rows, rows), 0) < iota((rows, rows), 1)).astype(BF16)
    base = jnp.zeros((tiles, 1), F32)
    out = []
    for k in range(top):
        here = dest[k : k + 1, :]
        hot = (iota((tiles, rows), 0) == here).astype(F32)
        ahead = dot32(hot.astype(BF16), upper) + base
        rank = jnp.sum(hot * ahead, axis=0, keepdims=True).astype(jnp.int32)
        base = base + jnp.sum(hot, axis=1, keepdims=True)
        out.append((hot, rank, here * CAP + rank))
    return out


def pack(tiles, geom, res_ref, chosen_ref, ft_ref, fb_ref, pay, cod, place_ref):
    cx, ny, nz = geom
    nzb = nz // 128
    per_layer = ny * nzb
    top, rows = ft_ref.shape
    sensors = chosen_ref.shape[0]
    lane = iota((1, rows), 1)
    keep = jnp.zeros((1, rows), jnp.int32)
    for i in range(sensors):
        keep = jnp.where(lane // (rows // sensors) == i, chosen_ref[i], keep)
    keep = keep.astype(F32)
    block = fb_ref[...]
    dest = ft_ref[...]
    layer = jnp.zeros_like(block)
    for i in range(1, cx):
        layer = layer + (block >= i * per_layer).astype(jnp.int32)
    in_layer = block - layer * per_layer
    y = in_layer // nzb
    zb = in_layer - y * nzb
    turned = cx - 1 - layer
    odd = dest % 2 == 1
    within = zb * plane_rows(geom) + 8 + y
    flats = (
        within + (cx + jnp.where(odd, turned, layer)) * pitch_of(geom),
        within + jnp.where(odd, layer, turned) * pitch_of(geom),
    )
    slots = slot_rows(dest, tiles)
    place = jnp.zeros((tiles * CAP, rows), F32)
    codes = [jnp.zeros((tiles, 128), F32) for _ in flats]
    for k, (hot, rank, slot) in enumerate(slots):
        place = place + (iota((tiles * CAP, rows), 0) == slot).astype(F32)
        at = (iota((128, rows), 0) == rank).astype(BF16)
        for o, flat in enumerate(flats):
            hi = (flat // 64).astype(F32)
            lo = (flat - flat // 64 * 64).astype(F32)
            upper = last_dims((hot * hi[k : k + 1]).astype(BF16), at)
            lower = last_dims((hot * lo[k : k + 1]).astype(BF16), at)
            codes[o] = codes[o] + upper * 64.0 + lower
    place_ref[...] = place.astype(BF16)
    payload = dot32((place * keep).astype(BF16), res_ref[...]).astype(BF16)
    codes = [c.astype(jnp.int32) for c in codes]
    for e in range(tiles):
        t = outer_of(e, tiles)
        pay[e, 0] = payload[e * CAP : e * CAP + CAP]
        cod[e, 0] = codes[0][e : e + 1]
        pay[e, 1] = jnp.zeros((CAP, 128), BF16) if t is None else payload[t * CAP : t * CAP + CAP]
        cod[e, 1] = jnp.zeros((1, 128), jnp.int32) if t is None else codes[1][t : t + 1]


def signal_all(n, me, partner):
    barrier = pltpu.get_barrier_semaphore()

    @pl.loop(1, n)
    def _(i):
        pl.semaphore_signal(barrier, inc=1, device_id={"tile": lax.rem(me + i, n)}, device_id_type=MESH)

    if partner is not None:
        pl.semaphore_signal(barrier, inc=1, device_id={"group": partner}, device_id_type=MESH)


def wait_all(n, partner):
    pl.semaphore_wait(pltpu.get_barrier_semaphore(), n - 1 if partner is None else n)


def where_am_i(n, groups):
    me = lax.axis_index("tile")
    odd = lax.rem(me, 2)
    nb = me + 2 * odd - 1
    inter = jnp.logical_and(nb >= 0, nb < n)
    if groups % 2:
        return me, odd, nb, inter, None, 0
    g = lax.axis_index("group")
    half = lax.rem(g, 2)
    return me, odd, nb, inter, g + 1 - 2 * half, half


class Halo:
    def __init__(self, source, target, sems, forward_sems, nb, partner, half):
        layers, ny = target.shape[0], target.shape[1]
        self.count = layers * CUTS
        self.paired = partner is not None
        size = (ny // 2 if self.paired else ny) // CUTS
        start = half * (ny // 2) if self.paired else 0

        def window(i):
            return i // CUTS, pl.ds(start + i % CUTS * size, size)

        def piece(i):
            return pltpu.make_async_remote_copy(
                source.at[window(i)], target.at[window(i)], sems.at[0, i], sems.at[1, i],
                device_id={"tile": nb}, device_id_type=MESH)

        def forward(i):
            here = target.at[window(i)]
            return pltpu.make_async_remote_copy(
                here, here, forward_sems.at[0, i], forward_sems.at[1, i],
                device_id={"group": partner}, device_id_type=MESH)

        self.piece, self.forward = piece, forward

    def start(self, i):
        self.piece(i).start()

    def hand_on(self, i):
        self.piece(i).wait_recv()
        if self.paired:
            self.forward(i).start()

    def arrived(self, i):
        if self.paired:
            self.forward(i).wait_recv()

    def sent(self, i):
        self.piece(i).wait_send()
        if self.paired:
            self.forward(i).wait_send()


def exchange_kernel(
    n, groups, geom, res_in, chosen_in, ft_in, fb_in, interp_in, speed_in,
    vals, gotc, u, rate, halo, later, place_ref,
    res_ref, chosen_ref, ft_ref, fb_ref, interp, first, pay, cod, got, nsem, ssem, sems, csems, isem, fsem, lsem
):
    cx, ny, nz = geom
    me, odd, nb, inter, partner, half = where_am_i(n, groups)
    signal_all(n, me, partner)
    loads = [
        pltpu.make_async_copy(speed_in.at[i + odd * (cx - 1 - 2 * i)], rate.at[i], ssem.at[i]) for i in range(cx)
    ]
    small = [
        pltpu.make_async_copy(a, b, nsem.at[i])
        for i, (a, b) in enumerate((
            (ft_in, ft_ref), (fb_in, fb_ref), (chosen_in, chosen_ref), (res_in, res_ref), (interp_in, interp)))
    ]
    for load in small + loads:
        load.start()
    for load in small:
        load.wait()
    pack(n, geom, res_ref, chosen_ref, ft_ref, fb_ref, pay, cod, place_ref)

    def scale(i):
        @pl.loop(0, ny // 16)
        def _(r):
            rows = pl.ds(pl.multiple_of(r * 16, 16), 16)
            new = RATE * rate[i, rows]
            rate[i, rows] = new
            if i < EARLY:
                first[i, rows] = new.astype(BF16)
            elif i < HALO:
                later[i - EARLY, rows] = new.astype(BF16)

    for i in range(EARLY):
        loads[i].wait()
        scale(i)
    wait_all(n, partner)

    def data(i):
        e = lax.rem(me + i, n)
        return pltpu.make_async_remote_copy(
            pay.at[e], got.at[me], sems.at[0, i], sems.at[1, i],
            device_id={"tile": e}, device_id_type=MESH)

    def code(i):
        e = lax.rem(me + i, n)
        return pltpu.make_async_remote_copy(
            cod.at[e], gotc.at[me], csems.at[0, i], csems.at[1, i],
            device_id={"tile": e}, device_id_type=MESH)

    beside = Halo(first, halo, isem, fsem, nb, partner, half)

    @pl.when(inter)
    def _():
        for i in range(beside.count):
            beside.start(i)

    @pl.loop(1, n)
    def _(i):
        data(i).start()
        code(i).start()

    own = pltpu.make_async_copy(pay.at[me], got.at[me], lsem.at[0])
    ownc = pltpu.make_async_copy(cod.at[me], gotc.at[me], lsem.at[1])
    own.start()
    ownc.start()

    zero = jnp.zeros((8, 128), F32)
    flat = u.shape[0]

    @pl.loop(0, flat // 128)
    def _(s):
        for i in range(16):
            u[pl.ds(pl.multiple_of(s * 128 + i * 8, 8), 8)] = zero

    for row in range(flat // 128 * 128, flat, 8):
        u[row : row + 8] = zero
    for i in range(EARLY, cx):
        loads[i].wait()
        scale(i)

    @pl.when(inter)
    def _():
        for i in range(beside.count):
            beside.hand_on(i)

    @pl.when(jnp.logical_not(inter))
    def _():
        halo[...] = jnp.zeros(halo.shape, halo.dtype)

    parts = jnp.concatenate(thirds(interp[...]), axis=1)

    size = 2 * CAP
    left, right = iota((size, size), 0), iota((size, size), 1)
    same, batch = left == right, left // BATCH == right // BATCH

    def inject(s):
        three = dot32(got[s].reshape(size, 128), parts)
        three = three[:, :128] + (three[:, 128:256] + three[:, 256:])
        across = jnp.concatenate([gotc[s, 0][:, :CAP], gotc[s, 1][:, :CAP]], axis=1)
        down = jnp.sum(jnp.where(same, across.astype(F32), 0.0), axis=1, keepdims=True)
        merge = jnp.logical_and(batch, down == across.astype(F32)).astype(BF16)
        three = dot32(merge, jnp.concatenate(thirds(three), axis=1))
        vals[s] = three[:, :128] + (three[:, 128:256] + three[:, 256:])

    own.wait()
    ownc.wait()
    inject(me)

    @pl.loop(1, n)
    def _(i):
        data(i).wait()
        code(i).wait()
        inject(lax.rem(me - i + n, n))

    @pl.when(inter)
    def _():
        for i in range(beside.count):
            beside.arrived(i)
            beside.sent(i)


def inject_kernel(codes, vals, u_in, u):
    @pl.loop(0, vals.shape[0])
    def _(s):
        for group in range(0, CAP, BATCH):
            rows = [(o, j) for j in range(group, group + BATCH) for o in range(2)]
            ats = [codes[s * 2 + o, j] for o, j in rows]
            new = [u[pl.ds(at, 1)] + vals[s, pl.ds(o * CAP + j, 1)] for at, (o, j) in zip(ats, rows)]
            for at, row in zip(ats, new):
                u[pl.ds(at, 1)] = row


def step_kernel(
    n, groups, geom, u0, codes, rate, halo, later, u4, ret, units,
    u1, u2, u3, edge, deep, taken, sampled, unit, isem, fsem, esem, sems, usems, lsem
):
    cx, ny, nz = geom
    nzb = nz // 128
    pitch = pitch_of(geom)
    plane = plane_rows(geom)
    me, odd, nb, inter, partner, half = where_am_i(n, groups)
    signal_all(n, me, partner)
    zero = jnp.zeros((8, 128), F32)
    for ref in (u1, u2, u3):
        for zb in range(nzb):
            for m in range(2 * cx + 1):
                ref[zb, m * pitch : m * pitch + 8] = zero
    u4[0:8] = zero

    @pl.when(jnp.logical_not(inter))
    def _():
        deep[...] = jnp.zeros(deep.shape, deep.dtype)

    wait_all(n, partner)
    last = 2 * cx - 1
    beside = Halo(later, deep, isem, fsem, nb, partner, half)

    def swap(src, step):
        return pltpu.make_async_remote_copy(
            src.at[:, pl.ds(last * pitch + 8, ny)], edge.at[step], esem.at[0, step], esem.at[1, step],
            device_id={"tile": me + 1 - 2 * odd}, device_id_type=MESH)

    swap(u0, 0).start()

    @pl.when(inter)
    def _():
        for i in range(beside.count):
            beside.start(i)

    lane = iota((BODY, 128), 1)
    first_lane, last_lane = lane == 0, lane == 127

    def step_rows(step, src, dst, lo, hi, row):
        base = row + 8

        def strip(m):
            if m > last:
                return [edge[step, zb, pl.ds(row, BODY)] for zb in range(nzb)]
            return [src[zb, pl.ds(base + m * pitch, BODY)] for zb in range(nzb)]

        below, here = strip(lo - 1), strip(lo)
        for m in range(lo, hi):
            above = strip(m + 1)
            for zb in range(nzb):
                lanes = slice(zb * 128, zb * 128 + 128)
                if m >= cx:
                    r = rate[m - cx, pl.ds(row, BODY), lanes]
                elif cx - 1 - m < EARLY:
                    r = halo[cx - 1 - m, pl.ds(row, BODY), lanes].astype(F32)
                else:
                    r = deep[cx - 1 - m - EARLY, pl.ds(row, BODY), lanes].astype(F32)
                c = here[zb]
                left = here[zb - 1] if zb > 0 else 0.0
                right = here[zb + 1] if zb + 1 < nzb else 0.0
                total = below[zb] + above[zb]
                total = total + (
                    src[zb, pl.ds(base + m * pitch - 1, BODY)] + src[zb, pl.ds(base + m * pitch + 1, BODY)])
                total = total + pltpu.roll(jnp.where(last_lane, left, c), 1, 1)
                total = total + pltpu.roll(jnp.where(first_lane, right, c), 127, 1)
                new = c + r * (total - 6.0 * c)
                if dst is u4:
                    dst[pl.ds(zb * plane + base + m * pitch, BODY)] = new
                else:
                    dst[zb, pl.ds(base + m * pitch, BODY)] = new
            below, here = here, above

    fields = (u0, u1, u2, u3, u4)

    def step(k, lo, hi):
        rows = ny // 2 if hi - lo > 1 else ny

        def part(start):
            for q in range(0, rows, BODY):
                step_rows(k, fields[k], fields[k + 1], lo, hi, start + q)

        if rows == ny:
            part(0)
        else:
            pl.loop(0, 2)(lambda p: part(pl.multiple_of(p * rows, BODY)))

    def close(k):
        swap(fields[k], k).wait_recv()
        step(k, last, last + 1)
        if k < STEPS - 1:
            swap(fields[k + 1], k + 1).start()

    def on_halo(act, first, count):
        @pl.when(inter)
        def _():
            for i in range(first, first + count):
                act(i)

    step(0, cx - 1, last)
    close(0)
    step(1, cx, last)
    on_halo(beside.hand_on, 0, 1)
    close(1)
    step(2, cx + 1, last)
    on_halo(beside.hand_on, 1, 1)
    close(2)
    step(3, cx + 2, last)
    on_halo(beside.hand_on, 2, 1)
    on_halo(beside.arrived, 0, CUTS)
    step(0, cx - 2, cx - 1)
    step(1, cx - 1, cx)
    step(2, cx, cx + 1)
    on_halo(beside.hand_on, 3, 1)
    step(3, cx + 1, cx + 2)
    close(3)
    on_halo(beside.arrived, CUTS, CUTS)
    step(0, cx - 3, cx - 2)
    step(1, cx - 2, cx - 1)
    step(2, cx - 1, cx)
    step(3, cx, cx + 1)

    def block(i):
        e = lax.rem(me + i, n)
        return pltpu.make_async_remote_copy(
            sampled.at[e], ret.at[me], sems.at[0, i], sems.at[1, i],
            device_id={"tile": e}, device_id_type=MESH)

    def sizes(i):
        e = lax.rem(me + i, n)
        return pltpu.make_async_remote_copy(
            unit.at[e], units.at[me], usems.at[0, i], usems.at[1, i],
            device_id={"tile": e}, device_id_type=MESH)

    diagonal = iota((CAP, 128), 0) == iota((CAP, 128), 1)

    def sample(e, i):
        for j in range(CAP):
            taken[i, pl.ds(j, 1)] = u4[pl.ds(codes[e * 2, j], 1)]

    def shrink(e, i):
        x = taken[i]
        top = jnp.maximum(jnp.max(jnp.abs(x), axis=1, keepdims=True), 1e-30)
        sampled[e] = jnp.round(x * (LEVELS / top)).astype(jnp.int32).astype(jnp.int16)
        unit[e] = jnp.sum(jnp.where(diagonal, top * (1.0 / LEVELS), 0.0), axis=0, keepdims=True)

    @pl.loop(1, n)
    def _(i):
        e = lax.rem(me + i, n)
        sample(e, i)
        shrink(e, i)
        block(i).start()
        sizes(i).start()

    sample(me, 0)
    shrink(me, 0)
    own = pltpu.make_async_copy(sampled.at[me], ret.at[me], lsem.at[0])
    ownu = pltpu.make_async_copy(unit.at[me], units.at[me], lsem.at[1])
    own.start()
    ownu.start()
    on_halo(beside.sent, 0, beside.count)
    for k in range(STEPS):
        swap(fields[k], k).wait_send()
    own.wait()
    ownu.wait()

    @pl.loop(1, n)
    def _(i):
        block(i).wait()
        sizes(i).wait()


def finish_kernel(geom, u4, ret, units, place, interp, field, out, blocks, sems):
    cx, ny, nz = geom
    pitch = pitch_of(geom)
    plane = plane_rows(geom)
    odd = lax.rem(lax.axis_index("tile"), 2)
    copies = [
        pltpu.make_async_copy(
            u4.at[pl.ds(zb * plane + (cx + i) * pitch + 8, ny)],
            field.at[i + odd * (cx - 1 - 2 * i), :, pl.ds(zb * 128, 128)],
            sems.at[i, zb])
        for i in range(cx) for zb in range(nz // 128)
    ]
    for copy in copies:
        copy.start()
    diagonal = iota((CAP, 128), 0) == iota((CAP, 128), 1)
    for s in range(ret.shape[0]):
        unit = jnp.sum(jnp.where(diagonal, units[s], 0.0), axis=1, keepdims=True)
        blocks[s] = ret[s].astype(jnp.int32).astype(F32) * unit
    parts = jnp.concatenate(thirds(blocks[...].reshape(-1, 128)), axis=1)
    three = lax.dot_general(place[...], parts, (((0,), (0,)), ((), ())), preferred_element_type=F32)
    total = three[:, :128] + (three[:, 128:256] + three[:, 256:])
    out[...] = lax.dot_general(
        total, interp[...], (((1,), (1,)), ((), ())), precision=HIGH, preferred_element_type=F32)
    for copy in copies:
        copy.wait()


def in_hbm(x):
    return pltpu.with_memory_space_constraint(x, pltpu.HBM)


def params(mib, **more):
    return pltpu.CompilerParams(vmem_limit_bytes=mib * 2**20, **more)


def body(groups, residual, chosen, footprint_tile, footprint_block, interp, speed):
    n = lax.axis_size("tile")
    cx, ny, nz = geom = speed.shape
    rows, samp = residual.shape
    nzb = nz // 128
    shape = jax.ShapeDtypeStruct
    dma = pltpu.SemaphoreType.DMA
    plane = plane_rows(geom)
    vals, codes, u0, rate, halo, later, place = pl.pallas_call(
        functools.partial(exchange_kernel, n, groups, geom),
        out_shape=(
            shape((n, 2 * CAP, samp), F32),
            shape((n, 2, 1, 128), jnp.int32),
            shape((nzb * plane, 128), F32),
            shape(geom, F32),
            shape((EARLY, ny, nz), BF16),
            shape((HALO - EARLY, ny, nz), BF16),
            shape((n * CAP, rows), BF16),
        ),
        in_specs=[HBM] * 6,
        out_specs=(VMEM,) * 7,
        scratch_shapes=[
            pltpu.VMEM((rows, samp), BF16), pltpu.SMEM(chosen.shape, jnp.int32),
            pltpu.VMEM(footprint_tile.shape[::-1], jnp.int32), pltpu.VMEM(footprint_tile.shape[::-1], jnp.int32),
            pltpu.VMEM((samp, samp), F32),
            pltpu.VMEM((EARLY, ny, nz), BF16),
            pltpu.VMEM((n, 2, CAP, samp), BF16), pltpu.VMEM((n, 2, 1, 128), jnp.int32),
            pltpu.VMEM((n, 2, CAP, samp), BF16),
            dma((5,)), dma((cx,)), dma((2, n)), dma((2, n)), dma((2, EARLY * CUTS)), dma((2, EARLY * CUTS)), dma((2,)),
        ],
        compiler_params=params(10, collective_id=0, has_side_effects=True),
        name="exchange",
    )(*(in_hbm(x) for x in (residual, chosen, footprint_tile.T, footprint_block.T, interp, speed)))
    codes = codes.reshape(n * 2, 128)
    u0 = pl.pallas_call(
        inject_kernel,
        out_shape=shape(u0.shape, F32),
        in_specs=[SMEM, VMEM, VMEM],
        out_specs=VMEM,
        input_output_aliases={2: 0},
        compiler_params=params(4),
        name="inject",
    )(codes, vals, u0)
    layers = pltpu.VMEM((nzb, plane, 128), F32)
    u4, ret, units = pl.pallas_call(
        functools.partial(step_kernel, n, groups, geom),
        out_shape=(
            shape((nzb * plane, 128), F32), shape((n, CAP, samp), jnp.int16), shape((n, 1, 128), F32)),
        in_specs=[VMEM, SMEM, VMEM, VMEM, VMEM],
        out_specs=(VMEM,) * 3,
        scratch_shapes=[
            layers, layers, layers,
            pltpu.VMEM((STEPS, nzb, ny, 128), F32), pltpu.VMEM((HALO - EARLY, ny, nz), BF16),
            pltpu.VMEM((n, CAP, samp), F32), pltpu.VMEM((n, CAP, samp), jnp.int16), pltpu.VMEM((n, 1, 128), F32),
            dma((2, (HALO - EARLY) * CUTS)), dma((2, (HALO - EARLY) * CUTS)), dma((2, STEPS)), dma((2, n)), dma((2, n)), dma((2,)),
        ],
        compiler_params=params(30, collective_id=1, has_side_effects=True),
        name="steps",
    )(u0.reshape(nzb, plane, 128), codes, rate, halo, later)
    return pl.pallas_call(
        functools.partial(finish_kernel, geom),
        out_shape=(shape(geom, F32), shape((rows, samp), F32)),
        in_specs=[VMEM] * 5,
        out_specs=(ANY, VMEM),
        scratch_shapes=[pltpu.VMEM((n, CAP, samp), F32), dma((cx, nzb))],
        compiler_params=params(8),
        name="finish",
    )(u4, ret, units, place, interp)


def solution(mesh):
    placed = (
        P(("group", "tile"), None),
        P(("group", "tile")),
        P("tile", None),
        P("tile", None),
        P(),
        P("tile", None, None),
    )
    return jax.shard_map(
        functools.partial(body, mesh.shape["group"]),
        mesh=mesh,
        in_specs=placed,
        out_specs=(P(("group", "tile"), None, None), P(("group", "tile"), None)),
        check_vma=False,
    )
```

```python
import functools

import jax
import jax.numpy as jnp
from jax import lax
from jax.experimental import pallas as pl
from jax.experimental.pallas import tpu as pltpu
from jax.sharding import PartitionSpec as P

CAP = 32
STEPS = 4
RATE = 0.16
HALO = STEPS - 1
CUTS = 2
EARLY = 1
TOGETHER = 3
BODY = 16
BATCH = 8
LEVELS = 32767.0
MESH = pl.DeviceIdType.MESH
VMEM = pl.BlockSpec(memory_space=pltpu.VMEM)
HBM = pl.BlockSpec(memory_space=pltpu.HBM)
ANY = pl.BlockSpec(memory_space=pl.ANY)
SMEM = pl.BlockSpec(memory_space=pltpu.SMEM)
F32 = jnp.float32
BF16 = jnp.bfloat16
HIGH = lax.Precision.HIGHEST


def iota(shape, dim):
    return lax.broadcasted_iota(jnp.int32, shape, dim)


def last_dims(a, b):
    return lax.dot_general(a, b, (((1,), (1,)), ((), ())), preferred_element_type=F32)


def dot32(a, b):
    return lax.dot_general(a, b, (((1,), (0,)), ((), ())), preferred_element_type=F32)


def pitch_of(geom):
    return geom[1] + 8


def plane_rows(geom):
    return 2 * geom[0] * pitch_of(geom) + 8


def outer_of(e, n):
    t = e - 1 if e % 2 == 0 else e + 1
    return t if 0 <= t < n else None


def thirds(x):
    a = x.astype(BF16)
    rest = x - a.astype(F32)
    b = rest.astype(BF16)
    return a, b, (rest - b.astype(F32)).astype(BF16)


def slot_rows(dest, tiles):
    top, rows = dest.shape
    upper = (iota((rows, rows), 0) < iota((rows, rows), 1)).astype(BF16)
    base = jnp.zeros((tiles, 1), F32)
    out = []
    for k in range(top):
        here = dest[k : k + 1, :]
        hot = (iota((tiles, rows), 0) == here).astype(F32)
        ahead = dot32(hot.astype(BF16), upper) + base
        rank = jnp.sum(hot * ahead, axis=0, keepdims=True).astype(jnp.int32)
        base = base + jnp.sum(hot, axis=1, keepdims=True)
        out.append((hot, rank, here * CAP + rank))
    return out


def pack(tiles, geom, res_ref, chosen_ref, ft_ref, fb_ref, pay, cod, place_ref):
    cx, ny, nz = geom
    nzb = nz // 128
    per_layer = ny * nzb
    top, rows = ft_ref.shape
    sensors = chosen_ref.shape[0]
    lane = iota((1, rows), 1)
    keep = jnp.zeros((1, rows), jnp.int32)
    for i in range(sensors):
        keep = jnp.where(lane // (rows // sensors) == i, chosen_ref[i], keep)
    keep = keep.astype(F32)
    block = fb_ref[...]
    dest = ft_ref[...]
    layer = jnp.zeros_like(block)
    for i in range(1, cx):
        layer = layer + (block >= i * per_layer).astype(jnp.int32)
    in_layer = block - layer * per_layer
    y = in_layer // nzb
    zb = in_layer - y * nzb
    turned = cx - 1 - layer
    odd = dest % 2 == 1
    within = zb * plane_rows(geom) + 8 + y
    flats = (
        within + (cx + jnp.where(odd, turned, layer)) * pitch_of(geom),
        within + jnp.where(odd, layer, turned) * pitch_of(geom),
    )
    slots = slot_rows(dest, tiles)
    place = jnp.zeros((tiles * CAP, rows), F32)
    codes = [jnp.zeros((tiles, 128), F32) for _ in flats]
    for k, (hot, rank, slot) in enumerate(slots):
        place = place + (iota((tiles * CAP, rows), 0) == slot).astype(F32)
        at = (iota((128, rows), 0) == rank).astype(BF16)
        for o, flat in enumerate(flats):
            hi = (flat // 64).astype(F32)
            lo = (flat - flat // 64 * 64).astype(F32)
            upper = last_dims((hot * hi[k : k + 1]).astype(BF16), at)
            lower = last_dims((hot * lo[k : k + 1]).astype(BF16), at)
            codes[o] = codes[o] + upper * 64.0 + lower
    place_ref[...] = place.astype(BF16)
    payload = dot32((place * keep).astype(BF16), res_ref[...]).astype(BF16)
    codes = [c.astype(jnp.int32) for c in codes]
    for e in range(tiles):
        t = outer_of(e, tiles)
        pay[e, 0] = payload[e * CAP : e * CAP + CAP]
        cod[e, 0] = codes[0][e : e + 1]
        pay[e, 1] = jnp.zeros((CAP, 128), BF16) if t is None else payload[t * CAP : t * CAP + CAP]
        cod[e, 1] = jnp.zeros((1, 128), jnp.int32) if t is None else codes[1][t : t + 1]


def signal_all(n, me, partner):
    barrier = pltpu.get_barrier_semaphore()

    @pl.loop(1, n)
    def _(i):
        pl.semaphore_signal(barrier, inc=1, device_id={"tile": lax.rem(me + i, n)}, device_id_type=MESH)

    if partner is not None:
        pl.semaphore_signal(barrier, inc=1, device_id={"group": partner}, device_id_type=MESH)


def wait_all(n, partner):
    pl.semaphore_wait(pltpu.get_barrier_semaphore(), n - 1 if partner is None else n)


def where_am_i(n, groups):
    me = lax.axis_index("tile")
    odd = lax.rem(me, 2)
    nb = me + 2 * odd - 1
    inter = jnp.logical_and(nb >= 0, nb < n)
    if groups % 2:
        return me, odd, nb, inter, None, 0
    g = lax.axis_index("group")
    half = lax.rem(g, 2)
    return me, odd, nb, inter, g + 1 - 2 * half, half


class Halo:
    def __init__(self, source, target, sems, forward_sems, nb, partner, half, alone):
        layers, ny = target.shape[0], target.shape[1]
        self.count = layers * CUTS
        paired = partner is not None
        size = (ny // 2 if paired else ny) // CUTS
        self.handed = self.count - alone if paired else 0
        self.both = paired

        def window(i, which):
            start = which * (ny // 2) if paired else 0
            return i // CUTS, pl.ds(start + i % CUTS * size, size)

        def straight(i, which, pair):
            at = window(i, which)
            return pltpu.make_async_remote_copy(
                source.at[at], target.at[at], pair.at[0, i], pair.at[1, i],
                device_id={"tile": nb}, device_id_type=MESH)

        def forward(i):
            here = target.at[window(i, half)]
            return pltpu.make_async_remote_copy(
                here, here, forward_sems.at[0, i], forward_sems.at[1, i],
                device_id={"group": partner}, device_id_type=MESH)

        self.piece = lambda i: straight(i, half, sems)
        self.second = lambda i: forward(i) if i < self.handed else straight(i, 1 - half, forward_sems)

    def start(self, i):
        self.piece(i).start()
        if self.both and i >= self.handed:
            self.second(i).start()

    def hand_on(self, i):
        if i < self.handed:
            self.piece(i).wait_recv()
            self.second(i).start()

    def arrived(self, i):
        if i >= self.handed:
            self.piece(i).wait_recv()
        if self.both:
            self.second(i).wait_recv()

    def sent(self, i):
        self.piece(i).wait_send()
        if self.both:
            self.second(i).wait_send()


def exchange_kernel(
    n, groups, geom, res_in, chosen_in, ft_in, fb_in, interp_in, speed_in,
    vals, gotc, u, rate, halo, later, place_ref,
    res_ref, chosen_ref, ft_ref, fb_ref, interp, first, pay, cod, got, nsem, ssem, sems, csems, isem, fsem, lsem
):
    cx, ny, nz = geom
    me, odd, nb, inter, partner, half = where_am_i(n, groups)
    signal_all(n, me, partner)
    loads = [
        pltpu.make_async_copy(speed_in.at[i + odd * (cx - 1 - 2 * i)], rate.at[i], ssem.at[i]) for i in range(cx)
    ]
    small = [
        pltpu.make_async_copy(a, b, nsem.at[i])
        for i, (a, b) in enumerate((
            (ft_in, ft_ref), (fb_in, fb_ref), (chosen_in, chosen_ref), (res_in, res_ref), (interp_in, interp)))
    ]
    for load in small + loads:
        load.start()
    for load in small:
        load.wait()
    pack(n, geom, res_ref, chosen_ref, ft_ref, fb_ref, pay, cod, place_ref)

    def scale(i):
        @pl.loop(0, ny // 16)
        def _(r):
            rows = pl.ds(pl.multiple_of(r * 16, 16), 16)
            new = RATE * rate[i, rows]
            rate[i, rows] = new
            if i < EARLY:
                first[i, rows] = new.astype(BF16)
            elif i < HALO:
                later[i - EARLY, rows] = new.astype(BF16)

    for i in range(EARLY):
        loads[i].wait()
        scale(i)
    wait_all(n, partner)

    def data(i):
        e = lax.rem(me + i, n)
        return pltpu.make_async_remote_copy(
            pay.at[e], got.at[me], sems.at[0, i], sems.at[1, i],
            device_id={"tile": e}, device_id_type=MESH)

    def code(i):
        e = lax.rem(me + i, n)
        return pltpu.make_async_remote_copy(
            cod.at[e], gotc.at[me], csems.at[0, i], csems.at[1, i],
            device_id={"tile": e}, device_id_type=MESH)

    beside = Halo(first, halo, isem, fsem, nb, partner, half, 0)

    @pl.when(inter)
    def _():
        for i in range(beside.count):
            beside.start(i)

    @pl.loop(1, n)
    def _(i):
        data(i).start()
        code(i).start()

    own = pltpu.make_async_copy(pay.at[me], got.at[me], lsem.at[0])
    ownc = pltpu.make_async_copy(cod.at[me], gotc.at[me], lsem.at[1])
    own.start()
    ownc.start()

    zero = jnp.zeros((8, 128), F32)
    flat = u.shape[0]

    @pl.loop(0, flat // 128)
    def _(s):
        for i in range(16):
            u[pl.ds(pl.multiple_of(s * 128 + i * 8, 8), 8)] = zero

    for row in range(flat // 128 * 128, flat, 8):
        u[row : row + 8] = zero
    for i in range(EARLY, cx):
        loads[i].wait()
        scale(i)

    @pl.when(inter)
    def _():
        for i in range(beside.count):
            beside.hand_on(i)

    @pl.when(jnp.logical_not(inter))
    def _():
        halo[...] = jnp.zeros(halo.shape, halo.dtype)

    parts = jnp.concatenate(thirds(interp[...]), axis=1)

    size = 2 * CAP
    left, right = iota((size, size), 0), iota((size, size), 1)
    same, batch = left == right, left // BATCH == right // BATCH

    def inject(s):
        three = dot32(got[s].reshape(size, 128), parts)
        three = three[:, :128] + (three[:, 128:256] + three[:, 256:])
        across = jnp.concatenate([gotc[s, 0][:, :CAP], gotc[s, 1][:, :CAP]], axis=1)
        down = jnp.sum(jnp.where(same, across.astype(F32), 0.0), axis=1, keepdims=True)
        merge = jnp.logical_and(batch, down == across.astype(F32)).astype(BF16)
        three = dot32(merge, jnp.concatenate(thirds(three), axis=1))
        vals[s] = three[:, :128] + (three[:, 128:256] + three[:, 256:])

    own.wait()
    ownc.wait()
    inject(me)

    together = TOGETHER if (n - 1) % TOGETHER == 0 else 1

    @pl.loop(0, (n - 1) // together)
    def _(p):
        some = [p * together + k + 1 for k in range(together)]
        for i in some:
            data(i).wait()
            code(i).wait()
        for i in some:
            inject(lax.rem(me - i + n, n))

    @pl.when(inter)
    def _():
        for i in range(beside.count):
            beside.arrived(i)
            beside.sent(i)


def inject_kernel(codes, vals, u_in, u):
    @pl.loop(0, vals.shape[0])
    def _(s):
        for group in range(0, CAP, BATCH):
            rows = [(o, j) for j in range(group, group + BATCH) for o in range(2)]
            ats = [codes[s * 2 + o, j] for o, j in rows]
            new = [u[pl.ds(at, 1)] + vals[s, pl.ds(o * CAP + j, 1)] for at, (o, j) in zip(ats, rows)]
            for at, row in zip(ats, new):
                u[pl.ds(at, 1)] = row


def step_kernel(
    n, groups, geom, u0, codes, rate, halo, later, u4, ret, units,
    u1, u2, u3, edge, deep, taken, sampled, unit, isem, fsem, esem, sems, usems, lsem
):
    cx, ny, nz = geom
    nzb = nz // 128
    pitch = pitch_of(geom)
    plane = plane_rows(geom)
    me, odd, nb, inter, partner, half = where_am_i(n, groups)
    signal_all(n, me, partner)
    zero = jnp.zeros((8, 128), F32)
    for ref in (u1, u2, u3):
        for zb in range(nzb):
            for m in range(2 * cx + 1):
                ref[zb, m * pitch : m * pitch + 8] = zero
    u4[0:8] = zero

    @pl.when(jnp.logical_not(inter))
    def _():
        deep[...] = jnp.zeros(deep.shape, deep.dtype)

    wait_all(n, partner)
    last = 2 * cx - 1
    beside = Halo(later, deep, isem, fsem, nb, partner, half, 1)

    def swap(src, step):
        return pltpu.make_async_remote_copy(
            src.at[:, pl.ds(last * pitch + 8, ny)], edge.at[step], esem.at[0, step], esem.at[1, step],
            device_id={"tile": me + 1 - 2 * odd}, device_id_type=MESH)

    swap(u0, 0).start()

    @pl.when(inter)
    def _():
        for i in range(beside.count):
            beside.start(i)

    lane = iota((BODY, 128), 1)
    first_lane, last_lane = lane == 0, lane == 127

    def step_rows(step, src, dst, lo, hi, row):
        base = row + 8

        def strip(m):
            if m > last:
                return [edge[step, zb, pl.ds(row, BODY)] for zb in range(nzb)]
            return [src[zb, pl.ds(base + m * pitch, BODY)] for zb in range(nzb)]

        below, here = strip(lo - 1), strip(lo)
        for m in range(lo, hi):
            above = strip(m + 1)
            for zb in range(nzb):
                lanes = slice(zb * 128, zb * 128 + 128)
                if m >= cx:
                    r = rate[m - cx, pl.ds(row, BODY), lanes]
                elif cx - 1 - m < EARLY:
                    r = halo[cx - 1 - m, pl.ds(row, BODY), lanes].astype(F32)
                else:
                    r = deep[cx - 1 - m - EARLY, pl.ds(row, BODY), lanes].astype(F32)
                c = here[zb]
                left = here[zb - 1] if zb > 0 else 0.0
                right = here[zb + 1] if zb + 1 < nzb else 0.0
                total = below[zb] + above[zb]
                total = total + (
                    src[zb, pl.ds(base + m * pitch - 1, BODY)] + src[zb, pl.ds(base + m * pitch + 1, BODY)])
                total = total + pltpu.roll(jnp.where(last_lane, left, c), 1, 1)
                total = total + pltpu.roll(jnp.where(first_lane, right, c), 127, 1)
                new = c + r * (total - 6.0 * c)
                if dst is u4:
                    dst[pl.ds(zb * plane + base + m * pitch, BODY)] = new
                else:
                    dst[zb, pl.ds(base + m * pitch, BODY)] = new
            below, here = here, above

    fields = (u0, u1, u2, u3, u4)

    def step(k, lo, hi):
        rows = ny // 2 if hi - lo > 1 else ny

        def part(start):
            for q in range(0, rows, BODY):
                step_rows(k, fields[k], fields[k + 1], lo, hi, start + q)

        if rows == ny:
            part(0)
        else:
            pl.loop(0, 2)(lambda p: part(pl.multiple_of(p * rows, BODY)))

    def close(k):
        swap(fields[k], k).wait_recv()
        step(k, last, last + 1)
        if k < STEPS - 1:
            swap(fields[k + 1], k + 1).start()

    def on_halo(act, first, count):
        @pl.when(inter)
        def _():
            for i in range(first, first + count):
                act(i)

    step(0, cx - 1, last)
    close(0)
    step(1, cx, last)
    on_halo(beside.hand_on, 0, 1)
    close(1)
    on_halo(beside.hand_on, 1, 1)
    step(2, cx + 1, last)
    on_halo(beside.hand_on, 2, 1)
    close(2)
    step(3, cx + 2, last)
    on_halo(beside.arrived, 0, CUTS)
    step(0, cx - 2, cx - 1)
    step(1, cx - 1, cx)
    step(2, cx, cx + 1)
    step(3, cx + 1, cx + 2)
    close(3)
    on_halo(beside.arrived, CUTS, CUTS)
    step(0, cx - 3, cx - 2)
    step(1, cx - 2, cx - 1)
    step(2, cx - 1, cx)
    step(3, cx, cx + 1)

    def block(i):
        e = lax.rem(me + i, n)
        return pltpu.make_async_remote_copy(
            sampled.at[e], ret.at[me], sems.at[0, i], sems.at[1, i],
            device_id={"tile": e}, device_id_type=MESH)

    def sizes(i):
        e = lax.rem(me + i, n)
        return pltpu.make_async_remote_copy(
            unit.at[e], units.at[me], usems.at[0, i], usems.at[1, i],
            device_id={"tile": e}, device_id_type=MESH)

    diagonal = iota((CAP, 128), 0) == iota((CAP, 128), 1)

    def sample(e, i):
        for j in range(CAP):
            taken[i, pl.ds(j, 1)] = u4[pl.ds(codes[e * 2, j], 1)]

    def shrink(e, i):
        x = taken[i]
        top = jnp.maximum(jnp.max(jnp.abs(x), axis=1, keepdims=True), 1e-30)
        sampled[e] = jnp.round(x * (LEVELS / top)).astype(jnp.int32).astype(jnp.int16)
        unit[e] = jnp.sum(jnp.where(diagonal, top * (1.0 / LEVELS), 0.0), axis=0, keepdims=True)

    together = TOGETHER if (n - 1) % TOGETHER == 0 else 1

    @pl.loop(0, (n - 1) // together)
    def _(p):
        some = [p * together + k + 1 for k in range(together)]
        for act in (sample, shrink):
            for i in some:
                act(lax.rem(me + i, n), i)
        for i in some:
            block(i).start()
            sizes(i).start()

    sample(me, 0)
    shrink(me, 0)
    own = pltpu.make_async_copy(sampled.at[me], ret.at[me], lsem.at[0])
    ownu = pltpu.make_async_copy(unit.at[me], units.at[me], lsem.at[1])
    own.start()
    ownu.start()
    on_halo(beside.sent, 0, beside.count)
    for k in range(STEPS):
        swap(fields[k], k).wait_send()
    own.wait()
    ownu.wait()

    @pl.loop(1, n)
    def _(i):
        block(i).wait()
        sizes(i).wait()


def finish_kernel(geom, u4, ret, units, place, interp, field, out, blocks, sems):
    cx, ny, nz = geom
    pitch = pitch_of(geom)
    plane = plane_rows(geom)
    odd = lax.rem(lax.axis_index("tile"), 2)
    copies = [
        pltpu.make_async_copy(
            u4.at[pl.ds(zb * plane + (cx + i) * pitch + 8, ny)],
            field.at[i + odd * (cx - 1 - 2 * i), :, pl.ds(zb * 128, 128)],
            sems.at[i, zb])
        for i in range(cx) for zb in range(nz // 128)
    ]
    for copy in copies:
        copy.start()
    diagonal = iota((CAP, 128), 0) == iota((CAP, 128), 1)
    for s in range(ret.shape[0]):
        unit = jnp.sum(jnp.where(diagonal, units[s], 0.0), axis=1, keepdims=True)
        blocks[s] = ret[s].astype(jnp.int32).astype(F32) * unit
    parts = jnp.concatenate(thirds(blocks[...].reshape(-1, 128)), axis=1)
    three = lax.dot_general(place[...], parts, (((0,), (0,)), ((), ())), preferred_element_type=F32)
    total = three[:, :128] + (three[:, 128:256] + three[:, 256:])
    out[...] = lax.dot_general(
        total, interp[...], (((1,), (1,)), ((), ())), precision=HIGH, preferred_element_type=F32)
    for copy in copies:
        copy.wait()


def in_hbm(x):
    return pltpu.with_memory_space_constraint(x, pltpu.HBM)


def params(mib, **more):
    return pltpu.CompilerParams(vmem_limit_bytes=mib * 2**20, **more)


def body(groups, residual, chosen, footprint_tile, footprint_block, interp, speed):
    n = lax.axis_size("tile")
    cx, ny, nz = geom = speed.shape
    rows, samp = residual.shape
    nzb = nz // 128
    shape = jax.ShapeDtypeStruct
    dma = pltpu.SemaphoreType.DMA
    plane = plane_rows(geom)
    vals, codes, u0, rate, halo, later, place = pl.pallas_call(
        functools.partial(exchange_kernel, n, groups, geom),
        out_shape=(
            shape((n, 2 * CAP, samp), F32),
            shape((n, 2, 1, 128), jnp.int32),
            shape((nzb * plane, 128), F32),
            shape(geom, F32),
            shape((EARLY, ny, nz), BF16),
            shape((HALO - EARLY, ny, nz), BF16),
            shape((n * CAP, rows), BF16),
        ),
        in_specs=[HBM] * 6,
        out_specs=(VMEM,) * 7,
        scratch_shapes=[
            pltpu.VMEM((rows, samp), BF16), pltpu.SMEM(chosen.shape, jnp.int32),
            pltpu.VMEM(footprint_tile.shape[::-1], jnp.int32), pltpu.VMEM(footprint_tile.shape[::-1], jnp.int32),
            pltpu.VMEM((samp, samp), F32),
            pltpu.VMEM((EARLY, ny, nz), BF16),
            pltpu.VMEM((n, 2, CAP, samp), BF16), pltpu.VMEM((n, 2, 1, 128), jnp.int32),
            pltpu.VMEM((n, 2, CAP, samp), BF16),
            dma((5,)), dma((cx,)), dma((2, n)), dma((2, n)), dma((2, EARLY * CUTS)), dma((2, EARLY * CUTS)), dma((2,)),
        ],
        compiler_params=params(10, collective_id=0, has_side_effects=True),
        name="exchange",
    )(*(in_hbm(x) for x in (residual, chosen, footprint_tile.T, footprint_block.T, interp, speed)))
    codes = codes.reshape(n * 2, 128)
    u0 = pl.pallas_call(
        inject_kernel,
        out_shape=shape(u0.shape, F32),
        in_specs=[SMEM, VMEM, VMEM],
        out_specs=VMEM,
        input_output_aliases={2: 0},
        compiler_params=params(4),
        name="inject",
    )(codes, vals, u0)
    layers = pltpu.VMEM((nzb, plane, 128), F32)
    u4, ret, units = pl.pallas_call(
        functools.partial(step_kernel, n, groups, geom),
        out_shape=(
            shape((nzb * plane, 128), F32), shape((n, CAP, samp), jnp.int16), shape((n, 1, 128), F32)),
        in_specs=[VMEM, SMEM, VMEM, VMEM, VMEM],
        out_specs=(VMEM,) * 3,
        scratch_shapes=[
            layers, layers, layers,
            pltpu.VMEM((STEPS, nzb, ny, 128), F32), pltpu.VMEM((HALO - EARLY, ny, nz), BF16),
            pltpu.VMEM((n, CAP, samp), F32), pltpu.VMEM((n, CAP, samp), jnp.int16), pltpu.VMEM((n, 1, 128), F32),
            dma((2, (HALO - EARLY) * CUTS)), dma((2, (HALO - EARLY) * CUTS)), dma((2, STEPS)), dma((2, n)), dma((2, n)), dma((2,)),
        ],
        compiler_params=params(30, collective_id=1, has_side_effects=True),
        name="steps",
    )(u0.reshape(nzb, plane, 128), codes, rate, halo, later)
    return pl.pallas_call(
        functools.partial(finish_kernel, geom),
        out_shape=(shape(geom, F32), shape((rows, samp), F32)),
        in_specs=[VMEM] * 5,
        out_specs=(ANY, VMEM),
        scratch_shapes=[pltpu.VMEM((n, CAP, samp), F32), dma((cx, nzb))],
        compiler_params=params(8),
        name="finish",
    )(u4, ret, units, place, interp)


def solution(mesh):
    placed = (
        P(("group", "tile"), None),
        P(("group", "tile")),
        P("tile", None),
        P("tile", None),
        P(),
        P("tile", None, None),
    )
    return jax.shard_map(
        functools.partial(body, mesh.shape["group"]),
        mesh=mesh,
        in_specs=placed,
        out_specs=(P(("group", "tile"), None, None), P(("group", "tile"), None)),
        check_vma=False,
    )
```

```python
import functools

import jax
import jax.numpy as jnp
from jax import lax
from jax.experimental import pallas as pl
from jax.experimental.pallas import tpu as pltpu
from jax.sharding import PartitionSpec as P

CAP = 32
STEPS = 4
RATE = 0.16
HALO = STEPS - 1
CUTS = 2
EARLY = 1
TOGETHER = 3
BODY = 16
BATCH = 8
LEVELS = 32767.0
MESH = pl.DeviceIdType.MESH
VMEM = pl.BlockSpec(memory_space=pltpu.VMEM)
HBM = pl.BlockSpec(memory_space=pltpu.HBM)
ANY = pl.BlockSpec(memory_space=pl.ANY)
SMEM = pl.BlockSpec(memory_space=pltpu.SMEM)
F32 = jnp.float32
BF16 = jnp.bfloat16
HIGH = lax.Precision.HIGHEST


def iota(shape, dim):
    return lax.broadcasted_iota(jnp.int32, shape, dim)


def last_dims(a, b):
    return lax.dot_general(a, b, (((1,), (1,)), ((), ())), preferred_element_type=F32)


def dot32(a, b):
    return lax.dot_general(a, b, (((1,), (0,)), ((), ())), preferred_element_type=F32)


def pitch_of(geom):
    return geom[1] + 8


def plane_rows(geom):
    return 2 * geom[0] * pitch_of(geom) + 8


def outer_of(e, n):
    t = e - 1 if e % 2 == 0 else e + 1
    return t if 0 <= t < n else None


def thirds(x):
    a = x.astype(BF16)
    rest = x - a.astype(F32)
    b = rest.astype(BF16)
    return a, b, (rest - b.astype(F32)).astype(BF16)


def slot_rows(dest, tiles):
    top, rows = dest.shape
    upper = (iota((rows, rows), 0) < iota((rows, rows), 1)).astype(BF16)
    base = jnp.zeros((tiles, 1), F32)
    out = []
    for k in range(top):
        here = dest[k : k + 1, :]
        hot = (iota((tiles, rows), 0) == here).astype(F32)
        ahead = dot32(hot.astype(BF16), upper) + base
        rank = jnp.sum(hot * ahead, axis=0, keepdims=True).astype(jnp.int32)
        base = base + jnp.sum(hot, axis=1, keepdims=True)
        out.append((hot, rank, here * CAP + rank))
    return out


def pack(tiles, geom, res_ref, chosen_ref, ft_ref, fb_ref, pay, cod, place_ref):
    cx, ny, nz = geom
    nzb = nz // 128
    per_layer = ny * nzb
    top, rows = ft_ref.shape
    sensors = chosen_ref.shape[0]
    lane = iota((1, rows), 1)
    keep = jnp.zeros((1, rows), jnp.int32)
    for i in range(sensors):
        keep = jnp.where(lane // (rows // sensors) == i, chosen_ref[i], keep)
    keep = keep.astype(F32)
    block = fb_ref[...]
    dest = ft_ref[...]
    layer = jnp.zeros_like(block)
    for i in range(1, cx):
        layer = layer + (block >= i * per_layer).astype(jnp.int32)
    in_layer = block - layer * per_layer
    y = in_layer // nzb
    zb = in_layer - y * nzb
    turned = cx - 1 - layer
    odd = dest % 2 == 1
    within = zb * plane_rows(geom) + 8 + y
    flats = (
        within + (cx + jnp.where(odd, turned, layer)) * pitch_of(geom),
        within + jnp.where(odd, layer, turned) * pitch_of(geom),
    )
    slots = slot_rows(dest, tiles)
    place = jnp.zeros((tiles * CAP, rows), F32)
    codes = [jnp.zeros((tiles, 128), F32) for _ in flats]
    for k, (hot, rank, slot) in enumerate(slots):
        place = place + (iota((tiles * CAP, rows), 0) == slot).astype(F32)
        at = (iota((128, rows), 0) == rank).astype(BF16)
        for o, flat in enumerate(flats):
            hi = (flat // 64).astype(F32)
            lo = (flat - flat // 64 * 64).astype(F32)
            upper = last_dims((hot * hi[k : k + 1]).astype(BF16), at)
            lower = last_dims((hot * lo[k : k + 1]).astype(BF16), at)
            codes[o] = codes[o] + upper * 64.0 + lower
    place_ref[...] = place.astype(BF16)
    payload = dot32((place * keep).astype(BF16), res_ref[...]).astype(BF16)
    codes = [c.astype(jnp.int32) for c in codes]
    for e in range(tiles):
        t = outer_of(e, tiles)
        pay[e, 0] = payload[e * CAP : e * CAP + CAP]
        cod[e, 0] = codes[0][e : e + 1]
        pay[e, 1] = jnp.zeros((CAP, 128), BF16) if t is None else payload[t * CAP : t * CAP + CAP]
        cod[e, 1] = jnp.zeros((1, 128), jnp.int32) if t is None else codes[1][t : t + 1]


def signal_all(n, me, partner):
    barrier = pltpu.get_barrier_semaphore()

    @pl.loop(1, n)
    def _(i):
        pl.semaphore_signal(barrier, inc=1, device_id={"tile": lax.rem(me + i, n)}, device_id_type=MESH)

    if partner is not None:
        pl.semaphore_signal(barrier, inc=1, device_id={"group": partner}, device_id_type=MESH)


def wait_all(n, partner):
    pl.semaphore_wait(pltpu.get_barrier_semaphore(), n - 1 if partner is None else n)


def where_am_i(n, groups):
    me = lax.axis_index("tile")
    odd = lax.rem(me, 2)
    nb = me + 2 * odd - 1
    inter = jnp.logical_and(nb >= 0, nb < n)
    if groups % 2:
        return me, odd, nb, inter, None, 0
    g = lax.axis_index("group")
    half = lax.rem(g, 2)
    return me, odd, nb, inter, g + 1 - 2 * half, half


class Halo:
    def __init__(self, source, target, sems, forward_sems, nb, partner, half, alone):
        layers, ny = target.shape[0], target.shape[1]
        self.count = layers * CUTS
        paired = partner is not None
        size = (ny // 2 if paired else ny) // CUTS
        self.handed = self.count - alone if paired else 0
        self.both = paired

        def window(i, which):
            start = which * (ny // 2) if paired else 0
            return i // CUTS, pl.ds(start + i % CUTS * size, size)

        def straight(i, which, pair):
            at = window(i, which)
            return pltpu.make_async_remote_copy(
                source.at[at], target.at[at], pair.at[0, i], pair.at[1, i],
                device_id={"tile": nb}, device_id_type=MESH)

        def forward(i):
            here = target.at[window(i, half)]
            return pltpu.make_async_remote_copy(
                here, here, forward_sems.at[0, i], forward_sems.at[1, i],
                device_id={"group": partner}, device_id_type=MESH)

        self.piece = lambda i: straight(i, half, sems)
        self.second = lambda i: forward(i) if i < self.handed else straight(i, 1 - half, forward_sems)

    def start(self, i):
        self.piece(i).start()
        if self.both and i >= self.handed:
            self.second(i).start()

    def hand_on(self, i):
        if i < self.handed:
            self.piece(i).wait_recv()
            self.second(i).start()

    def arrived(self, i):
        if i >= self.handed:
            self.piece(i).wait_recv()
        if self.both:
            self.second(i).wait_recv()

    def sent(self, i):
        self.piece(i).wait_send()
        if self.both:
            self.second(i).wait_send()


def exchange_kernel(
    n, groups, geom, res_in, chosen_in, ft_in, fb_in, interp_in, speed_in,
    vals, gotc, u, rate, halo, later, place_ref,
    res_ref, chosen_ref, ft_ref, fb_ref, interp, first, pay, cod, got, nsem, ssem, sems, csems, isem, fsem, lsem
):
    cx, ny, nz = geom
    me, odd, nb, inter, partner, half = where_am_i(n, groups)
    signal_all(n, me, partner)
    loads = [
        pltpu.make_async_copy(speed_in.at[i + odd * (cx - 1 - 2 * i)], rate.at[i], ssem.at[i]) for i in range(cx)
    ]
    small = [
        pltpu.make_async_copy(a, b, nsem.at[i])
        for i, (a, b) in enumerate((
            (ft_in, ft_ref), (fb_in, fb_ref), (chosen_in, chosen_ref), (res_in, res_ref), (interp_in, interp)))
    ]
    for load in small + loads:
        load.start()
    for load in small:
        load.wait()
    pack(n, geom, res_ref, chosen_ref, ft_ref, fb_ref, pay, cod, place_ref)

    def scale(i):
        @pl.loop(0, ny // 16)
        def _(r):
            rows = pl.ds(pl.multiple_of(r * 16, 16), 16)
            new = RATE * rate[i, rows]
            rate[i, rows] = new
            if i < EARLY:
                first[i, rows] = new.astype(BF16)
            elif i < HALO:
                later[i - EARLY, rows] = new.astype(BF16)

    for i in range(EARLY):
        loads[i].wait()
        scale(i)
    wait_all(n, partner)

    def data(i):
        e = lax.rem(me + i, n)
        return pltpu.make_async_remote_copy(
            pay.at[e], got.at[me], sems.at[0, i], sems.at[1, i],
            device_id={"tile": e}, device_id_type=MESH)

    def code(i):
        e = lax.rem(me + i, n)
        return pltpu.make_async_remote_copy(
            cod.at[e], gotc.at[me], csems.at[0, i], csems.at[1, i],
            device_id={"tile": e}, device_id_type=MESH)

    beside = Halo(first, halo, isem, fsem, nb, partner, half, 0)

    @pl.when(inter)
    def _():
        for i in range(beside.count):
            beside.start(i)

    @pl.loop(1, n)
    def _(i):
        data(i).start()
        code(i).start()

    own = pltpu.make_async_copy(pay.at[me], got.at[me], lsem.at[0])
    ownc = pltpu.make_async_copy(cod.at[me], gotc.at[me], lsem.at[1])
    own.start()
    ownc.start()

    zero = jnp.zeros((8, 128), F32)
    flat = u.shape[0]

    @pl.loop(0, flat // 128)
    def _(s):
        for i in range(16):
            u[pl.ds(pl.multiple_of(s * 128 + i * 8, 8), 8)] = zero

    for row in range(flat // 128 * 128, flat, 8):
        u[row : row + 8] = zero
    for i in range(EARLY, cx):
        loads[i].wait()
        scale(i)

    @pl.when(inter)
    def _():
        for i in range(beside.count):
            beside.hand_on(i)

    @pl.when(jnp.logical_not(inter))
    def _():
        halo[...] = jnp.zeros(halo.shape, halo.dtype)

    parts = jnp.concatenate(thirds(interp[...]), axis=1)

    size = 2 * CAP
    left, right = iota((size, size), 0), iota((size, size), 1)
    same, batch = left == right, left // BATCH == right // BATCH

    def inject(s):
        three = dot32(got[s].reshape(size, 128), parts)
        three = three[:, :128] + (three[:, 128:256] + three[:, 256:])
        across = jnp.concatenate([gotc[s, 0][:, :CAP], gotc[s, 1][:, :CAP]], axis=1)
        down = jnp.sum(jnp.where(same, across.astype(F32), 0.0), axis=1, keepdims=True)
        merge = jnp.logical_and(batch, down == across.astype(F32)).astype(BF16)
        three = dot32(merge, jnp.concatenate(thirds(three), axis=1))
        vals[s] = three[:, :128] + (three[:, 128:256] + three[:, 256:])

    own.wait()
    ownc.wait()
    inject(me)

    together = TOGETHER if (n - 1) % TOGETHER == 0 else 1

    @pl.loop(0, (n - 1) // together)
    def _(p):
        some = [p * together + k + 1 for k in range(together)]
        for i in some:
            data(i).wait()
            code(i).wait()
        for i in some:
            inject(lax.rem(me - i + n, n))

    @pl.when(inter)
    def _():
        for i in range(beside.count):
            beside.arrived(i)
            beside.sent(i)


def inject_kernel(codes, vals, u_in, u):
    @pl.loop(0, vals.shape[0])
    def _(s):
        for group in range(0, CAP, BATCH):
            rows = [(o, j) for j in range(group, group + BATCH) for o in range(2)]
            ats = [codes[s * 2 + o, j] for o, j in rows]
            new = [u[pl.ds(at, 1)] + vals[s, pl.ds(o * CAP + j, 1)] for at, (o, j) in zip(ats, rows)]
            for at, row in zip(ats, new):
                u[pl.ds(at, 1)] = row


def step_kernel(
    n, groups, geom, u0, codes, rate, halo, later, u4, ret, units,
    u1, u2, u3, edge, parts, deep, taken, sampled, unit, isem, fsem, esem, sems, usems, lsem
):
    cx, ny, nz = geom
    nzb = nz // 128
    pitch = pitch_of(geom)
    plane = plane_rows(geom)
    me, odd, nb, inter, partner, half = where_am_i(n, groups)
    signal_all(n, me, partner)
    zero = jnp.zeros((8, 128), F32)
    for ref in (u1, u2, u3):
        for zb in range(nzb):
            for m in range(2 * cx + 1):
                ref[zb, m * pitch : m * pitch + 8] = zero
    u4[0:8] = zero

    @pl.loop(0, ny // 8)
    def _(p):
        for zb in range(nzb):
            u1[zb, pl.ds(pl.multiple_of(p * 8, 8) + 8 + (cx - HALO) * pitch, 8)] = zero

    @pl.when(jnp.logical_not(inter))
    def _():
        deep[...] = jnp.zeros(deep.shape, deep.dtype)

    wait_all(n, partner)
    last = 2 * cx - 1
    beside = Halo(later, deep, isem, fsem, nb, partner, half, 1)

    def swap(src, step):
        return pltpu.make_async_remote_copy(
            src.at[:, pl.ds(last * pitch + 8, ny)], edge.at[step], esem.at[0, step], esem.at[1, step],
            device_id={"tile": me + 1 - 2 * odd}, device_id_type=MESH)

    swap(u0, 0).start()

    @pl.when(inter)
    def _():
        for i in range(beside.count):
            beside.start(i)

    lane = iota((BODY, 128), 1)
    first_lane, last_lane = lane == 0, lane == 127

    def rate_at(m, row, lanes):
        if m >= cx:
            return rate[m - cx, pl.ds(row, BODY), lanes]
        d = cx - 1 - m
        r = halo[d, pl.ds(row, BODY), lanes] if d < EARLY else deep[d - EARLY, pl.ds(row, BODY), lanes]
        return r.astype(F32)

    def around(src, row, m, zb, below, here, above):
        at = row + 8 + m * pitch
        c = here[zb]
        left = here[zb - 1] if zb > 0 else 0.0
        right = here[zb + 1] if zb + 1 < nzb else 0.0
        total = below[zb] + above[zb]
        total = total + (src[zb, pl.ds(at - 1, BODY)] + src[zb, pl.ds(at + 1, BODY)])
        total = total + pltpu.roll(jnp.where(last_lane, left, c), 1, 1)
        total = total + pltpu.roll(jnp.where(first_lane, right, c), 127, 1)
        return c, total - 6.0 * c

    far = cx - HALO

    def prepare():
        for row in range(0, ny, BODY):
            strips = [[u0[zb, pl.ds(row + 8 + m * pitch, BODY)] for zb in range(nzb)] for m in range(far - 1, far + 2)]
            for zb in range(nzb):
                lanes = slice(zb * 128, zb * 128 + 128)
                c, pull = around(u0, row, far, zb, *strips)
                path = rate_at(cx, row, lanes)
                for m in range(far + 1, cx):
                    path = path * rate_at(m, row, lanes)
                parts[0, pl.ds(row, BODY), lanes] = path * c
                parts[1, pl.ds(row, BODY), lanes] = path * pull

    def complete():
        for row in range(0, ny, BODY):
            for zb in range(nzb):
                lanes = slice(zb * 128, zb * 128 + 128)
                at = pl.ds(zb * plane + row + 8 + cx * pitch, BODY)
                more = parts[0, pl.ds(row, BODY), lanes] + rate_at(far, row, lanes) * parts[1, pl.ds(row, BODY), lanes]
                u4[at] = u4[at] + more

    def step_rows(step, src, dst, lo, hi, row):
        base = row + 8

        def strip(m):
            if m > last:
                return [edge[step, zb, pl.ds(row, BODY)] for zb in range(nzb)]
            return [src[zb, pl.ds(base + m * pitch, BODY)] for zb in range(nzb)]

        below, here = strip(lo - 1), strip(lo)
        for m in range(lo, hi):
            above = strip(m + 1)
            for zb in range(nzb):
                lanes = slice(zb * 128, zb * 128 + 128)
                c, pull = around(src, row, m, zb, below, here, above)
                new = c + rate_at(m, row, lanes) * pull
                if dst is u4:
                    dst[pl.ds(zb * plane + base + m * pitch, BODY)] = new
                else:
                    dst[zb, pl.ds(base + m * pitch, BODY)] = new
            below, here = here, above

    fields = (u0, u1, u2, u3, u4)

    def step(k, lo, hi):
        rows = ny // 2 if hi - lo > 1 else ny

        def part(start):
            for q in range(0, rows, BODY):
                step_rows(k, fields[k], fields[k + 1], lo, hi, start + q)

        if rows == ny:
            part(0)
        else:
            pl.loop(0, 2)(lambda p: part(pl.multiple_of(p * rows, BODY)))

    def close(k):
        swap(fields[k], k).wait_recv()
        step(k, last, last + 1)
        if k < STEPS - 1:
            swap(fields[k + 1], k + 1).start()

    def on_halo(act, first, count):
        @pl.when(inter)
        def _():
            for i in range(first, first + count):
                act(i)

    step(0, cx - 1, last)
    close(0)
    step(1, cx, last)
    on_halo(beside.hand_on, 0, 1)
    close(1)
    on_halo(beside.hand_on, 1, 1)
    step(2, cx + 1, last)
    on_halo(beside.hand_on, 2, 1)
    close(2)
    step(3, cx + 2, last)
    on_halo(beside.arrived, 0, CUTS)
    step(0, cx - 2, cx - 1)
    step(1, cx - 1, cx)
    step(2, cx, cx + 1)
    step(3, cx + 1, cx + 2)
    close(3)
    prepare()
    step(1, cx - 2, cx - 1)
    step(2, cx - 1, cx)
    step(3, cx, cx + 1)
    on_halo(beside.arrived, CUTS, CUTS)
    complete()

    def block(i):
        e = lax.rem(me + i, n)
        return pltpu.make_async_remote_copy(
            sampled.at[e], ret.at[me], sems.at[0, i], sems.at[1, i],
            device_id={"tile": e}, device_id_type=MESH)

    def sizes(i):
        e = lax.rem(me + i, n)
        return pltpu.make_async_remote_copy(
            unit.at[e], units.at[me], usems.at[0, i], usems.at[1, i],
            device_id={"tile": e}, device_id_type=MESH)

    diagonal = iota((CAP, 128), 0) == iota((CAP, 128), 1)

    def sample(e, i):
        for j in range(CAP):
            taken[i, pl.ds(j, 1)] = u4[pl.ds(codes[e * 2, j], 1)]

    def shrink(e, i):
        x = taken[i]
        top = jnp.maximum(jnp.max(jnp.abs(x), axis=1, keepdims=True), 1e-30)
        sampled[e] = jnp.round(x * (LEVELS / top)).astype(jnp.int32).astype(jnp.int16)
        unit[e] = jnp.sum(jnp.where(diagonal, top * (1.0 / LEVELS), 0.0), axis=0, keepdims=True)

    together = TOGETHER if (n - 1) % TOGETHER == 0 else 1

    @pl.loop(0, (n - 1) // together)
    def _(p):
        some = [p * together + k + 1 for k in range(together)]
        for act in (sample, shrink):
            for i in some:
                act(lax.rem(me + i, n), i)
        for i in some:
            block(i).start()
            sizes(i).start()

    sample(me, 0)
    shrink(me, 0)
    own = pltpu.make_async_copy(sampled.at[me], ret.at[me], lsem.at[0])
    ownu = pltpu.make_async_copy(unit.at[me], units.at[me], lsem.at[1])
    own.start()
    ownu.start()
    on_halo(beside.sent, 0, beside.count)
    for k in range(STEPS):
        swap(fields[k], k).wait_send()
    own.wait()
    ownu.wait()

    @pl.loop(1, n)
    def _(i):
        block(i).wait()
        sizes(i).wait()


def finish_kernel(geom, u4, ret, units, place, interp, field, out, blocks, sems):
    cx, ny, nz = geom
    pitch = pitch_of(geom)
    plane = plane_rows(geom)
    odd = lax.rem(lax.axis_index("tile"), 2)
    copies = [
        pltpu.make_async_copy(
            u4.at[pl.ds(zb * plane + (cx + i) * pitch + 8, ny)],
            field.at[i + odd * (cx - 1 - 2 * i), :, pl.ds(zb * 128, 128)],
            sems.at[i, zb])
        for i in range(cx) for zb in range(nz // 128)
    ]
    for copy in copies:
        copy.start()
    diagonal = iota((CAP, 128), 0) == iota((CAP, 128), 1)
    for s in range(ret.shape[0]):
        unit = jnp.sum(jnp.where(diagonal, units[s], 0.0), axis=1, keepdims=True)
        blocks[s] = ret[s].astype(jnp.int32).astype(F32) * unit
    parts = jnp.concatenate(thirds(blocks[...].reshape(-1, 128)), axis=1)
    three = lax.dot_general(place[...], parts, (((0,), (0,)), ((), ())), preferred_element_type=F32)
    total = three[:, :128] + (three[:, 128:256] + three[:, 256:])
    out[...] = lax.dot_general(
        total, interp[...], (((1,), (1,)), ((), ())), precision=HIGH, preferred_element_type=F32)
    for copy in copies:
        copy.wait()


def in_hbm(x):
    return pltpu.with_memory_space_constraint(x, pltpu.HBM)


def params(mib, **more):
    return pltpu.CompilerParams(vmem_limit_bytes=mib * 2**20, **more)


def body(groups, residual, chosen, footprint_tile, footprint_block, interp, speed):
    n = lax.axis_size("tile")
    cx, ny, nz = geom = speed.shape
    rows, samp = residual.shape
    nzb = nz // 128
    shape = jax.ShapeDtypeStruct
    dma = pltpu.SemaphoreType.DMA
    plane = plane_rows(geom)
    vals, codes, u0, rate, halo, later, place = pl.pallas_call(
        functools.partial(exchange_kernel, n, groups, geom),
        out_shape=(
            shape((n, 2 * CAP, samp), F32),
            shape((n, 2, 1, 128), jnp.int32),
            shape((nzb * plane, 128), F32),
            shape(geom, F32),
            shape((EARLY, ny, nz), BF16),
            shape((HALO - EARLY, ny, nz), BF16),
            shape((n * CAP, rows), BF16),
        ),
        in_specs=[HBM] * 6,
        out_specs=(VMEM,) * 7,
        scratch_shapes=[
            pltpu.VMEM((rows, samp), BF16), pltpu.SMEM(chosen.shape, jnp.int32),
            pltpu.VMEM(footprint_tile.shape[::-1], jnp.int32), pltpu.VMEM(footprint_tile.shape[::-1], jnp.int32),
            pltpu.VMEM((samp, samp), F32),
            pltpu.VMEM((EARLY, ny, nz), BF16),
            pltpu.VMEM((n, 2, CAP, samp), BF16), pltpu.VMEM((n, 2, 1, 128), jnp.int32),
            pltpu.VMEM((n, 2, CAP, samp), BF16),
            dma((5,)), dma((cx,)), dma((2, n)), dma((2, n)), dma((2, EARLY * CUTS)), dma((2, EARLY * CUTS)), dma((2,)),
        ],
        compiler_params=params(10, collective_id=0, has_side_effects=True),
        name="exchange",
    )(*(in_hbm(x) for x in (residual, chosen, footprint_tile.T, footprint_block.T, interp, speed)))
    codes = codes.reshape(n * 2, 128)
    u0 = pl.pallas_call(
        inject_kernel,
        out_shape=shape(u0.shape, F32),
        in_specs=[SMEM, VMEM, VMEM],
        out_specs=VMEM,
        input_output_aliases={2: 0},
        compiler_params=params(4),
        name="inject",
    )(codes, vals, u0)
    layers = pltpu.VMEM((nzb, plane, 128), F32)
    u4, ret, units = pl.pallas_call(
        functools.partial(step_kernel, n, groups, geom),
        out_shape=(
            shape((nzb * plane, 128), F32), shape((n, CAP, samp), jnp.int16), shape((n, 1, 128), F32)),
        in_specs=[VMEM, SMEM, VMEM, VMEM, VMEM],
        out_specs=(VMEM,) * 3,
        scratch_shapes=[
            layers, layers, layers,
            pltpu.VMEM((STEPS, nzb, ny, 128), F32), pltpu.VMEM((2, ny, nz), F32), pltpu.VMEM((HALO - EARLY, ny, nz), BF16),
            pltpu.VMEM((n, CAP, samp), F32), pltpu.VMEM((n, CAP, samp), jnp.int16), pltpu.VMEM((n, 1, 128), F32),
            dma((2, (HALO - EARLY) * CUTS)), dma((2, (HALO - EARLY) * CUTS)), dma((2, STEPS)), dma((2, n)), dma((2, n)), dma((2,)),
        ],
        compiler_params=params(34, collective_id=1, has_side_effects=True),
        name="steps",
    )(u0.reshape(nzb, plane, 128), codes, rate, halo, later)
    return pl.pallas_call(
        functools.partial(finish_kernel, geom),
        out_shape=(shape(geom, F32), shape((rows, samp), F32)),
        in_specs=[VMEM] * 5,
        out_specs=(ANY, VMEM),
        scratch_shapes=[pltpu.VMEM((n, CAP, samp), F32), dma((cx, nzb))],
        compiler_params=params(8),
        name="finish",
    )(u4, ret, units, place, interp)


def solution(mesh):
    placed = (
        P(("group", "tile"), None),
        P(("group", "tile")),
        P("tile", None),
        P("tile", None),
        P(),
        P("tile", None, None),
    )
    return jax.shard_map(
        functools.partial(body, mesh.shape["group"]),
        mesh=mesh,
        in_specs=placed,
        out_specs=(P(("group", "tile"), None, None), P(("group", "tile"), None)),
        check_vma=False,
    )
```

```python
import functools

import jax
import jax.numpy as jnp
from jax import lax
from jax.experimental import pallas as pl
from jax.experimental.pallas import tpu as pltpu
from jax.sharding import PartitionSpec as P

CAP = 32
STEPS = 4
RATE = 0.16
HALO = STEPS - 1
CUTS = 2
EARLY = 2
FIRST = -(-EARLY // CUTS)
SHARED = EARLY // CUTS
TOGETHER = 3
BODY = 16
BATCH = 8
LEVELS = 32767.0
MESH = pl.DeviceIdType.MESH
VMEM = pl.BlockSpec(memory_space=pltpu.VMEM)
HBM = pl.BlockSpec(memory_space=pltpu.HBM)
ANY = pl.BlockSpec(memory_space=pl.ANY)
SMEM = pl.BlockSpec(memory_space=pltpu.SMEM)
F32 = jnp.float32
BF16 = jnp.bfloat16
HIGH = lax.Precision.HIGHEST


def iota(shape, dim):
    return lax.broadcasted_iota(jnp.int32, shape, dim)


def last_dims(a, b):
    return lax.dot_general(a, b, (((1,), (1,)), ((), ())), preferred_element_type=F32)


def dot32(a, b):
    return lax.dot_general(a, b, (((1,), (0,)), ((), ())), preferred_element_type=F32)


def pitch_of(geom):
    return geom[1] + 8


def plane_rows(geom):
    return 2 * geom[0] * pitch_of(geom) + 8


def outer_of(e, n):
    t = e - 1 if e % 2 == 0 else e + 1
    return t if 0 <= t < n else None


def thirds(x):
    a = x.astype(BF16)
    rest = x - a.astype(F32)
    b = rest.astype(BF16)
    return a, b, (rest - b.astype(F32)).astype(BF16)


def slot_rows(dest, tiles):
    top, rows = dest.shape
    upper = (iota((rows, rows), 0) < iota((rows, rows), 1)).astype(BF16)
    base = jnp.zeros((tiles, 1), F32)
    out = []
    for k in range(top):
        here = dest[k : k + 1, :]
        hot = (iota((tiles, rows), 0) == here).astype(F32)
        ahead = dot32(hot.astype(BF16), upper) + base
        rank = jnp.sum(hot * ahead, axis=0, keepdims=True).astype(jnp.int32)
        base = base + jnp.sum(hot, axis=1, keepdims=True)
        out.append((hot, rank, here * CAP + rank))
    return out


def pack(tiles, geom, res_ref, chosen_ref, ft_ref, fb_ref, pay, cod, place_ref):
    cx, ny, nz = geom
    nzb = nz // 128
    per_layer = ny * nzb
    top, rows = ft_ref.shape
    sensors = chosen_ref.shape[0]
    lane = iota((1, rows), 1)
    keep = jnp.zeros((1, rows), jnp.int32)
    for i in range(sensors):
        keep = jnp.where(lane // (rows // sensors) == i, chosen_ref[i], keep)
    keep = keep.astype(F32)
    block = fb_ref[...]
    dest = ft_ref[...]
    layer = jnp.zeros_like(block)
    for i in range(1, cx):
        layer = layer + (block >= i * per_layer).astype(jnp.int32)
    in_layer = block - layer * per_layer
    y = in_layer // nzb
    zb = in_layer - y * nzb
    turned = cx - 1 - layer
    odd = dest % 2 == 1
    within = zb * plane_rows(geom) + 8 + y
    flats = (
        within + (cx + jnp.where(odd, turned, layer)) * pitch_of(geom),
        within + jnp.where(odd, layer, turned) * pitch_of(geom),
    )
    slots = slot_rows(dest, tiles)
    place = jnp.zeros((tiles * CAP, rows), F32)
    codes = [jnp.zeros((tiles, 128), F32) for _ in flats]
    for k, (hot, rank, slot) in enumerate(slots):
        place = place + (iota((tiles * CAP, rows), 0) == slot).astype(F32)
        at = (iota((128, rows), 0) == rank).astype(BF16)
        for o, flat in enumerate(flats):
            hi = (flat // 64).astype(F32)
            lo = (flat - flat // 64 * 64).astype(F32)
            upper = last_dims((hot * hi[k : k + 1]).astype(BF16), at)
            lower = last_dims((hot * lo[k : k + 1]).astype(BF16), at)
            codes[o] = codes[o] + upper * 64.0 + lower
    place_ref[...] = place.astype(BF16)
    payload = dot32((place * keep).astype(BF16), res_ref[...]).astype(BF16)
    codes = [c.astype(jnp.int32) for c in codes]
    for e in range(tiles):
        t = outer_of(e, tiles)
        pay[e, 0] = payload[e * CAP : e * CAP + CAP]
        cod[e, 0] = codes[0][e : e + 1]
        pay[e, 1] = jnp.zeros((CAP, 128), BF16) if t is None else payload[t * CAP : t * CAP + CAP]
        cod[e, 1] = jnp.zeros((1, 128), jnp.int32) if t is None else codes[1][t : t + 1]


def signal_all(n, me, partner):
    barrier = pltpu.get_barrier_semaphore()

    @pl.loop(1, n)
    def _(i):
        pl.semaphore_signal(barrier, inc=1, device_id={"tile": lax.rem(me + i, n)}, device_id_type=MESH)

    if partner is not None:
        pl.semaphore_signal(barrier, inc=1, device_id={"group": partner}, device_id_type=MESH)


def wait_all(n, partner):
    pl.semaphore_wait(pltpu.get_barrier_semaphore(), n - 1 if partner is None else n)


def where_am_i(n, groups):
    me = lax.axis_index("tile")
    odd = lax.rem(me, 2)
    nb = me + 2 * odd - 1
    inter = jnp.logical_and(nb >= 0, nb < n)
    if groups % 2:
        return me, odd, nb, inter, None, 0
    g = lax.axis_index("group")
    half = lax.rem(g, 2)
    return me, odd, nb, inter, g + 1 - 2 * half, half


class Halo:
    def __init__(self, source, target, base, pieces, sems, forward_sems, nb, partner, half, alone):
        ny = target.shape[1]
        self.pieces = pieces
        paired = partner is not None
        size = (ny // 2 if paired else ny) // CUTS
        self.handed = pieces[-1] + 1 - alone if paired else 0
        self.both = paired

        def window(i, which):
            start = which * (ny // 2) if paired else 0
            return i // CUTS - base, pl.ds(start + i % CUTS * size, size)

        def straight(i, which, pair):
            at = window(i, which)
            return pltpu.make_async_remote_copy(
                source.at[at], target.at[at], pair.at[0, i - pieces[0]], pair.at[1, i - pieces[0]],
                device_id={"tile": nb}, device_id_type=MESH)

        def forward(i):
            here = target.at[window(i, half)]
            return pltpu.make_async_remote_copy(
                here, here, forward_sems.at[0, i - pieces[0]], forward_sems.at[1, i - pieces[0]],
                device_id={"group": partner}, device_id_type=MESH)

        self.piece = lambda i: straight(i, half, sems)
        self.second = lambda i: forward(i) if i < self.handed else straight(i, 1 - half, forward_sems)

    def start(self, i):
        self.piece(i).start()
        if self.both and i >= self.handed:
            self.second(i).start()

    def hand_on(self, i):
        if i < self.handed:
            self.piece(i).wait_recv()
            self.second(i).start()

    def arrived(self, i):
        if i >= self.handed:
            self.piece(i).wait_recv()
        if self.both:
            self.second(i).wait_recv()

    def sent(self, i):
        self.piece(i).wait_send()
        if self.both:
            self.second(i).wait_send()


def exchange_kernel(
    n, groups, geom, res_in, chosen_in, ft_in, fb_in, interp_in, speed_in,
    vals, gotc, u, rate, halo, later, place_ref,
    res_ref, chosen_ref, ft_ref, fb_ref, interp, first, pay, cod, got, nsem, ssem, sems, csems, isem, fsem, lsem
):
    cx, ny, nz = geom
    me, odd, nb, inter, partner, half = where_am_i(n, groups)
    signal_all(n, me, partner)
    loads = [
        pltpu.make_async_copy(speed_in.at[i + odd * (cx - 1 - 2 * i)], rate.at[i], ssem.at[i]) for i in range(cx)
    ]
    small = [
        pltpu.make_async_copy(a, b, nsem.at[i])
        for i, (a, b) in enumerate((
            (ft_in, ft_ref), (fb_in, fb_ref), (chosen_in, chosen_ref), (res_in, res_ref), (interp_in, interp)))
    ]
    for load in small + loads:
        load.start()
    for load in small:
        load.wait()
    pack(n, geom, res_ref, chosen_ref, ft_ref, fb_ref, pay, cod, place_ref)

    def scale(i):
        @pl.loop(0, ny // 16)
        def _(r):
            rows = pl.ds(pl.multiple_of(r * 16, 16), 16)
            new = RATE * rate[i, rows]
            rate[i, rows] = new
            if i < FIRST:
                first[i, rows] = new.astype(BF16)
            if SHARED <= i < HALO:
                later[i - SHARED, rows] = new.astype(BF16)

    for i in range(FIRST):
        loads[i].wait()
        scale(i)
    wait_all(n, partner)

    def data(i):
        e = lax.rem(me + i, n)
        return pltpu.make_async_remote_copy(
            pay.at[e], got.at[me], sems.at[0, i], sems.at[1, i],
            device_id={"tile": e}, device_id_type=MESH)

    def code(i):
        e = lax.rem(me + i, n)
        return pltpu.make_async_remote_copy(
            cod.at[e], gotc.at[me], csems.at[0, i], csems.at[1, i],
            device_id={"tile": e}, device_id_type=MESH)

    beside = Halo(first, halo, 0, range(EARLY), isem, fsem, nb, partner, half, 0)

    @pl.when(inter)
    def _():
        for i in beside.pieces:
            beside.start(i)

    @pl.loop(1, n)
    def _(i):
        data(i).start()
        code(i).start()

    own = pltpu.make_async_copy(pay.at[me], got.at[me], lsem.at[0])
    ownc = pltpu.make_async_copy(cod.at[me], gotc.at[me], lsem.at[1])
    own.start()
    ownc.start()

    zero = jnp.zeros((8, 128), F32)
    flat = u.shape[0]

    @pl.loop(0, flat // 128)
    def _(s):
        for i in range(16):
            u[pl.ds(pl.multiple_of(s * 128 + i * 8, 8), 8)] = zero

    for row in range(flat // 128 * 128, flat, 8):
        u[row : row + 8] = zero
    for i in range(FIRST, cx):
        loads[i].wait()
        scale(i)

    @pl.when(inter)
    def _():
        for i in beside.pieces:
            beside.hand_on(i)

    @pl.when(jnp.logical_not(inter))
    def _():
        halo[...] = jnp.zeros(halo.shape, halo.dtype)

    parts = jnp.concatenate(thirds(interp[...]), axis=1)

    size = 2 * CAP
    left, right = iota((size, size), 0), iota((size, size), 1)
    same, batch = left == right, left // BATCH == right // BATCH

    def inject(s):
        three = dot32(got[s].reshape(size, 128), parts)
        three = three[:, :128] + (three[:, 128:256] + three[:, 256:])
        across = jnp.concatenate([gotc[s, 0][:, :CAP], gotc[s, 1][:, :CAP]], axis=1)
        down = jnp.sum(jnp.where(same, across.astype(F32), 0.0), axis=1, keepdims=True)
        merge = jnp.logical_and(batch, down == across.astype(F32)).astype(BF16)
        three = dot32(merge, jnp.concatenate(thirds(three), axis=1))
        vals[s] = three[:, :128] + (three[:, 128:256] + three[:, 256:])

    own.wait()
    ownc.wait()
    inject(me)

    together = TOGETHER if (n - 1) % TOGETHER == 0 else 1

    @pl.loop(0, (n - 1) // together)
    def _(p):
        some = [p * together + k + 1 for k in range(together)]
        for i in some:
            data(i).wait()
            code(i).wait()
        for i in some:
            inject(lax.rem(me - i + n, n))

    @pl.when(inter)
    def _():
        for i in beside.pieces:
            beside.arrived(i)
            beside.sent(i)


def inject_kernel(codes, vals, u_in, u):
    @pl.loop(0, vals.shape[0])
    def _(s):
        for group in range(0, CAP, BATCH):
            rows = [(o, j) for j in range(group, group + BATCH) for o in range(2)]
            ats = [codes[s * 2 + o, j] for o, j in rows]
            new = [u[pl.ds(at, 1)] + vals[s, pl.ds(o * CAP + j, 1)] for at, (o, j) in zip(ats, rows)]
            for at, row in zip(ats, new):
                u[pl.ds(at, 1)] = row


def step_kernel(
    n, groups, geom, u0, codes, rate, halo, later, u4, ret, units,
    u1, u2, u3, give, edge, deep, taken, sampled, unit, isem, fsem, esem, sems, usems, lsem
):
    cx, ny, nz = geom
    nzb = nz // 128
    pitch = pitch_of(geom)
    plane = plane_rows(geom)
    me, odd, nb, inter, partner, half = where_am_i(n, groups)
    signal_all(n, me, partner)
    zero = jnp.zeros((8, 128), F32)
    for ref in (u1, u2, u3):
        for zb in range(nzb):
            for m in range(2 * cx + 1):
                ref[zb, m * pitch : m * pitch + 8] = zero
    u4[0:8] = zero

    @pl.when(jnp.logical_not(inter))
    def _():
        deep[...] = jnp.zeros(deep.shape, deep.dtype)

    last = 2 * cx - 1

    @pl.loop(0, ny // 16)
    def _(p):
        row = pl.multiple_of(p * 16, 16)
        for zb in range(nzb):
            give[0, pl.ds(row, 16), zb * 128 : zb * 128 + 128] = u0[zb, pl.ds(row + last * pitch + 8, 16)].astype(BF16)

    wait_all(n, partner)
    beside = Halo(later, deep, SHARED, range(EARLY, HALO * CUTS), isem, fsem, nb, partner, half, 1)

    def swap(step):
        return pltpu.make_async_remote_copy(
            give.at[step], edge.at[step], esem.at[0, step], esem.at[1, step],
            device_id={"tile": me + 1 - 2 * odd}, device_id_type=MESH)

    swap(0).start()

    @pl.when(inter)
    def _():
        for i in beside.pieces:
            beside.start(i)

    span = ny if partner is None else ny // 2
    lane = iota((BODY, 128), 1)
    first_lane, last_lane = lane == 0, lane == 127

    def step_rows(step, src, dst, lo, hi, row):
        base = row + 8

        def strip(m):
            if m > last:
                return [edge[step, pl.ds(row, BODY), zb * 128 : zb * 128 + 128].astype(F32) for zb in range(nzb)]
            return [src[zb, pl.ds(base + m * pitch, BODY)] for zb in range(nzb)]

        below, here = strip(lo - 1), strip(lo)
        for m in range(lo, hi):
            above = strip(m + 1)
            for zb in range(nzb):
                lanes = slice(zb * 128, zb * 128 + 128)
                if m >= cx:
                    r = rate[m - cx, pl.ds(row, BODY), lanes]
                else:
                    d = cx - 1 - m
                    came = d < SHARED or (d < FIRST and row % span // (span // CUTS) + d * CUTS < EARLY)
                    r = halo[d, pl.ds(row, BODY), lanes] if came else deep[d - SHARED, pl.ds(row, BODY), lanes]
                    r = r.astype(F32)
                c = here[zb]
                left = here[zb - 1] if zb > 0 else 0.0
                right = here[zb + 1] if zb + 1 < nzb else 0.0
                total = below[zb] + above[zb]
                total = total + (
                    src[zb, pl.ds(base + m * pitch - 1, BODY)] + src[zb, pl.ds(base + m * pitch + 1, BODY)])
                total = total + pltpu.roll(jnp.where(last_lane, left, c), 1, 1)
                total = total + pltpu.roll(jnp.where(first_lane, right, c), 127, 1)
                new = c + r * (total - 6.0 * c)
                if dst is u4:
                    dst[pl.ds(zb * plane + base + m * pitch, BODY)] = new
                else:
                    dst[zb, pl.ds(base + m * pitch, BODY)] = new
                    if m == last:
                        give[step + 1, pl.ds(row, BODY), lanes] = new.astype(BF16)
            below, here = here, above

    fields = (u0, u1, u2, u3, u4)

    def step(k, lo, hi):
        rows = ny // 2 if hi - lo > 1 else ny

        def part(start):
            for q in range(0, rows, BODY):
                step_rows(k, fields[k], fields[k + 1], lo, hi, start + q)

        if rows == ny:
            part(0)
        else:
            pl.loop(0, 2)(lambda p: part(pl.multiple_of(p * rows, BODY)))

    def close(k):
        swap(k).wait_recv()
        step(k, last, last + 1)
        if k < STEPS - 1:
            swap(k + 1).start()

    def on_halo(act, pieces):
        @pl.when(inter)
        def _():
            for i in pieces:
                act(i)

    step(0, cx - 1, last)
    close(0)
    on_halo(beside.hand_on, [2])
    step(1, cx, last)
    on_halo(beside.hand_on, [3])
    close(1)
    step(2, cx + 1, last)
    on_halo(beside.hand_on, [4])
    close(2)
    step(3, cx + 2, last)
    on_halo(beside.arrived, [2, 3])
    step(0, cx - 2, cx - 1)
    step(1, cx - 1, cx)
    step(2, cx, cx + 1)
    step(3, cx + 1, cx + 2)
    close(3)
    on_halo(beside.arrived, [4, 5])
    step(0, cx - 3, cx - 2)
    step(1, cx - 2, cx - 1)
    step(2, cx - 1, cx)
    step(3, cx, cx + 1)

    def block(i):
        e = lax.rem(me + i, n)
        return pltpu.make_async_remote_copy(
            sampled.at[e], ret.at[me], sems.at[0, i], sems.at[1, i],
            device_id={"tile": e}, device_id_type=MESH)

    def sizes(i):
        e = lax.rem(me + i, n)
        return pltpu.make_async_remote_copy(
            unit.at[e], units.at[me], usems.at[0, i], usems.at[1, i],
            device_id={"tile": e}, device_id_type=MESH)

    diagonal = iota((CAP, 128), 0) == iota((CAP, 128), 1)

    def sample(e, i):
        for j in range(CAP):
            taken[i, pl.ds(j, 1)] = u4[pl.ds(codes[e * 2, j], 1)]

    def shrink(e, i):
        x = taken[i]
        top = jnp.maximum(jnp.max(jnp.abs(x), axis=1, keepdims=True), 1e-30)
        sampled[e] = jnp.round(x * (LEVELS / top)).astype(jnp.int32).astype(jnp.int16)
        unit[e] = jnp.sum(jnp.where(diagonal, top * (1.0 / LEVELS), 0.0), axis=0, keepdims=True)

    together = TOGETHER if (n - 1) % TOGETHER == 0 else 1

    @pl.loop(0, (n - 1) // together)
    def _(p):
        some = [p * together + k + 1 for k in range(together)]
        for act in (sample, shrink):
            for i in some:
                act(lax.rem(me + i, n), i)
        for i in some:
            block(i).start()
            sizes(i).start()

    sample(me, 0)
    shrink(me, 0)
    own = pltpu.make_async_copy(sampled.at[me], ret.at[me], lsem.at[0])
    ownu = pltpu.make_async_copy(unit.at[me], units.at[me], lsem.at[1])
    own.start()
    ownu.start()
    on_halo(beside.sent, beside.pieces)
    for k in range(STEPS):
        swap(k).wait_send()
    own.wait()
    ownu.wait()

    @pl.loop(1, n)
    def _(i):
        block(i).wait()
        sizes(i).wait()


def finish_kernel(geom, u4, ret, units, place, interp, field, out, blocks, sems):
    cx, ny, nz = geom
    pitch = pitch_of(geom)
    plane = plane_rows(geom)
    odd = lax.rem(lax.axis_index("tile"), 2)
    copies = [
        pltpu.make_async_copy(
            u4.at[pl.ds(zb * plane + (cx + i) * pitch + 8, ny)],
            field.at[i + odd * (cx - 1 - 2 * i), :, pl.ds(zb * 128, 128)],
            sems.at[i, zb])
        for i in range(cx) for zb in range(nz // 128)
    ]
    for copy in copies:
        copy.start()
    diagonal = iota((CAP, 128), 0) == iota((CAP, 128), 1)
    for s in range(ret.shape[0]):
        unit = jnp.sum(jnp.where(diagonal, units[s], 0.0), axis=1, keepdims=True)
        blocks[s] = ret[s].astype(jnp.int32).astype(F32) * unit
    parts = jnp.concatenate(thirds(blocks[...].reshape(-1, 128)), axis=1)
    three = lax.dot_general(place[...], parts, (((0,), (0,)), ((), ())), preferred_element_type=F32)
    total = three[:, :128] + (three[:, 128:256] + three[:, 256:])
    out[...] = lax.dot_general(
        total, interp[...], (((1,), (1,)), ((), ())), precision=HIGH, preferred_element_type=F32)
    for copy in copies:
        copy.wait()


def in_hbm(x):
    return pltpu.with_memory_space_constraint(x, pltpu.HBM)


def params(mib, **more):
    return pltpu.CompilerParams(vmem_limit_bytes=mib * 2**20, **more)


def body(groups, residual, chosen, footprint_tile, footprint_block, interp, speed):
    n = lax.axis_size("tile")
    cx, ny, nz = geom = speed.shape
    rows, samp = residual.shape
    nzb = nz // 128
    shape = jax.ShapeDtypeStruct
    dma = pltpu.SemaphoreType.DMA
    plane = plane_rows(geom)
    vals, codes, u0, rate, halo, later, place = pl.pallas_call(
        functools.partial(exchange_kernel, n, groups, geom),
        out_shape=(
            shape((n, 2 * CAP, samp), F32),
            shape((n, 2, 1, 128), jnp.int32),
            shape((nzb * plane, 128), F32),
            shape(geom, F32),
            shape((FIRST, ny, nz), BF16),
            shape((HALO - SHARED, ny, nz), BF16),
            shape((n * CAP, rows), BF16),
        ),
        in_specs=[HBM] * 6,
        out_specs=(VMEM,) * 7,
        scratch_shapes=[
            pltpu.VMEM((rows, samp), BF16), pltpu.SMEM(chosen.shape, jnp.int32),
            pltpu.VMEM(footprint_tile.shape[::-1], jnp.int32), pltpu.VMEM(footprint_tile.shape[::-1], jnp.int32),
            pltpu.VMEM((samp, samp), F32),
            pltpu.VMEM((FIRST, ny, nz), BF16),
            pltpu.VMEM((n, 2, CAP, samp), BF16), pltpu.VMEM((n, 2, 1, 128), jnp.int32),
            pltpu.VMEM((n, 2, CAP, samp), BF16),
            dma((5,)), dma((cx,)), dma((2, n)), dma((2, n)), dma((2, EARLY)), dma((2, EARLY)), dma((2,)),
        ],
        compiler_params=params(10, collective_id=0, has_side_effects=True),
        name="exchange",
    )(*(in_hbm(x) for x in (residual, chosen, footprint_tile.T, footprint_block.T, interp, speed)))
    codes = codes.reshape(n * 2, 128)
    u0 = pl.pallas_call(
        inject_kernel,
        out_shape=shape(u0.shape, F32),
        in_specs=[SMEM, VMEM, VMEM],
        out_specs=VMEM,
        input_output_aliases={2: 0},
        compiler_params=params(4),
        name="inject",
    )(codes, vals, u0)
    layers = pltpu.VMEM((nzb, plane, 128), F32)
    u4, ret, units = pl.pallas_call(
        functools.partial(step_kernel, n, groups, geom),
        out_shape=(
            shape((nzb * plane, 128), F32), shape((n, CAP, samp), jnp.int16), shape((n, 1, 128), F32)),
        in_specs=[VMEM, SMEM, VMEM, VMEM, VMEM],
        out_specs=(VMEM,) * 3,
        scratch_shapes=[
            layers, layers, layers,
            pltpu.VMEM((STEPS, ny, nz), BF16), pltpu.VMEM((STEPS, ny, nz), BF16), pltpu.VMEM((HALO - SHARED, ny, nz), BF16),
            pltpu.VMEM((n, CAP, samp), F32), pltpu.VMEM((n, CAP, samp), jnp.int16), pltpu.VMEM((n, 1, 128), F32),
            dma((2, HALO * CUTS - EARLY)), dma((2, HALO * CUTS - EARLY)), dma((2, STEPS)), dma((2, n)), dma((2, n)), dma((2,)),
        ],
        compiler_params=params(30, collective_id=1, has_side_effects=True),
        name="steps",
    )(u0.reshape(nzb, plane, 128), codes, rate, halo, later)
    return pl.pallas_call(
        functools.partial(finish_kernel, geom),
        out_shape=(shape(geom, F32), shape((rows, samp), F32)),
        in_specs=[VMEM] * 5,
        out_specs=(ANY, VMEM),
        scratch_shapes=[pltpu.VMEM((n, CAP, samp), F32), dma((cx, nzb))],
        compiler_params=params(8),
        name="finish",
    )(u4, ret, units, place, interp)


def solution(mesh):
    placed = (
        P(("group", "tile"), None),
        P(("group", "tile")),
        P("tile", None),
        P("tile", None),
        P(),
        P("tile", None, None),
    )
    return jax.shard_map(
        functools.partial(body, mesh.shape["group"]),
        mesh=mesh,
        in_specs=placed,
        out_specs=(P(("group", "tile"), None, None), P(("group", "tile"), None)),
        check_vma=False,
    )
```
